256 devices in a mesh: dp: 64 (over z, y, x_hi), strip: 4 (over x_lo, core).
Axes of the slice: x: 4 (x_hi: 2, x_lo: 2; x = x_hi * 2 + x_lo), y: 4, z: 8, core: 2. Of those that a mesh axis runs over, the one named last changes fastest.
Arguments:
- images: bfloat16 [256, 3, 32, 128], P('dp', None, 'strip'), may hold values from -16 to 16
- perturbation: float32 [3, 32, 128], P(None, 'strip'), may hold values from -0.5 to 0.5
- labels: int32 [256], P(('dp', 'strip')), may hold values from 0 to 61
- step_levels: int32 [3], replicated, may hold values from 1 to 4
- stem_weight: bfloat16 [48, 192], replicated, may hold values from -0.875 to 0.875
- stem_gain: float32 [192], replicated, may hold values from 0.25 to 1.75
- dw1_kernel: bfloat16 [49, 192], replicated, may hold values from -0.875 to 0.875
- norm1_gain: float32 [192], replicated, may hold values from 0.25 to 1.75
- up1_weight: bfloat16 [192, 768], replicated, may hold values from -0.4375 to 0.4375
- down1_weight: bfloat16 [768, 192], replicated, may hold values from -0.21875 to 0.21875
- scale1: float32 [192], replicated, may hold values from 0.3 to 1
- down_gain: float32 [192], replicated, may hold values from 0.25 to 1.75
- ds_weight: bfloat16 [768, 384], replicated, may hold values from -0.21875 to 0.21875
- head_gain: float32 [384], replicated, may hold values from 0.25 to 1.75
- head_weight: bfloat16 [384, 62], replicated, may hold values from -0.3125 to 0.3125
Outputs:
- new_perturbation: float32 [3, 32, 128], P(None, 'strip')
- losses: float32 [256], P(('dp', 'strip'))
- stem_grad: float32 [48, 192], P(None, 'dp')
- dw1_grad: float32 [49, 192], P(None, 'dp')
- up1_grad: float32 [192, 768], P(None, 'dp')
- down1_grad: float32 [768, 192], P('dp')
- ds_grad: float32 [768, 384], P(None, 'dp')
- head_grad: float32 [384, 62], P('dp')
The draws below stay inside these ranges and needn't reach their ends.
All inputs are finite; a program needn't handle non-finite values.
Results may differ from the reference program's by a relative error of at most 0.013.
Values may be sent and summed in bfloat16 or wider, within the bound.
A program may use at most 64 MiB of HBM per device.

```python
import math
import jax
import jax.numpy as jnp
from jax import lax

C1 = 192
F1 = 768
C2 = 384
KS = 7
PATCH = 4
CLASSES = 62
IMAGES = 256
PIX_ROWS = 32
PIX_COLS = 128


def draw_images(key, part):
    shape_all = (IMAGES, 3, PIX_ROWS, PIX_COLS)
    fraction = jnp.arange(PIX_ROWS, dtype=jnp.float32) / PIX_ROWS
    base = jnp.clip(jax.random.normal(key, shape_all, jnp.float32), -4.0, 4.0)
    upper_scale = 3.0
    lower_scale = 0.3
    row_scale = upper_scale * jnp.exp(jnp.log(lower_scale / upper_scale) * fraction)
    return (base * row_scale[None, None, :, None]).astype(jnp.bfloat16)


def set_ends(array, key, low, top_value):
    longest = array.shape.index(max(array.shape))
    spots = []
    for shift in (0, 1):
        where = [jax.random.randint(jax.random.fold_in(key, axis), (), 0, length) for axis, length in enumerate(array.shape)]
        where[longest] = (where[longest] + shift) % array.shape[longest]
        spots.append(tuple(where))
    return array.at[spots[0]].set(low).at[spots[1]].set(top_value)


def shard_levels(own_key, extent, split, smallest, high):
    loudness = 1.0
    for dim, parts in split:
        steps = jax.random.uniform(jax.random.fold_in(jax.random.fold_in(own_key, 6), dim), (parts,), jnp.float32, smallest / len(split), high / len(split))
        loudness = loudness * jnp.repeat(jnp.exp(steps), extent[dim] // parts).reshape((-1,) + (1,) * (len(extent) - 1 - dim))
    return loudness


def bell_draw(stream_key, shape, scale, most, held_as=jnp.bfloat16):
    return jnp.clip(scale * jax.random.normal(stream_key, shape, jnp.float32), -most, most).astype(held_as)


def setup_inputs(seed: int = 0) -> dict:
    splits = jax.random.split(jax.random.key(seed), 16)
    return {
        "images": draw_images(jax.random.fold_in(splits[15], 71), 0),
        "perturbation": jnp.clip(jax.random.uniform(splits[1], (3, PIX_ROWS, PIX_COLS), jnp.float32, -0.5, 0.5) * shard_levels(splits[1], (3, PIX_ROWS, PIX_COLS), ((1, 4),), -0.4, 0.0), -0.5, 0.5),
        "labels": set_ends(jax.random.randint(splits[2], (IMAGES,), 0, CLASSES), jax.random.fold_in(splits[2], 1), 0, CLASSES - 1).astype(jnp.int32),
        "step_levels": jax.random.randint(splits[3], (3,), 1, 5).astype(jnp.int32),
        "stem_weight": bell_draw(splits[4], (3 * PATCH * PATCH, C1), (3 * PATCH * PATCH) ** -0.5, 0.875),
        "stem_gain": jnp.clip(1.0 + 0.15 * jax.random.normal(splits[5], (C1,), jnp.float32), 0.25, 1.75),
        "dw1_kernel": bell_draw(splits[6], (KS * KS, C1), (KS * KS) ** -0.5, 0.875),
        "norm1_gain": jnp.clip(1.0 + 0.15 * jax.random.normal(splits[7], (C1,), jnp.float32), 0.25, 1.75),
        "up1_weight": bell_draw(splits[8], (C1, F1), C1 ** -0.5, 0.4375),
        "down1_weight": bell_draw(splits[9], (F1, C1), F1 ** -0.5, 0.21875),
        "scale1": jnp.clip(jnp.exp(jax.random.uniform(splits[10], (C1,), jnp.float32, math.log(0.3), math.log(1.0))), 0.3, 1.0),
        "down_gain": jnp.clip(1.0 + 0.15 * jax.random.normal(splits[11], (C1,), jnp.float32), 0.25, 1.75),
        "ds_weight": bell_draw(splits[12], (4 * C1, C2), (4 * C1) ** -0.5, 0.21875),
        "head_gain": jnp.clip(1.0 + 0.15 * jax.random.normal(splits[13], (C2,), jnp.float32), 0.25, 1.75),
        "head_weight": bell_draw(splits[14], (C2, CLASSES), C2 ** -0.5, 0.3125),
    }


EPS_NORM = 1e-06
EPS_ROOT = 1e-12
BOUND = 0.5
STEP_UNIT = 0.1

def norm_gain(values_in, gain_vec):
    centre = lax.optimization_barrier(jnp.mean(values_in, axis=-1, keepdims=True))
    centred = values_in - centre
    spread = lax.optimization_barrier(jnp.mean(centred * centred, axis=-1, keepdims=True))
    return centred * lax.rsqrt(spread + EPS_NORM) * gain_vec

def norm_back(values_in, gain_vec, grad_out):

    def apply_norm(argument):
        return norm_gain(argument, gain_vec)
    return jax.vjp(apply_norm, values_in)[1](grad_out)[0]

def dense(values_in, weight):
    flattened = values_in.astype(jnp.bfloat16).reshape(-1, values_in.shape[-1])
    result = jnp.dot(flattened, weight, preferred_element_type=jnp.float32)
    return result.reshape(values_in.shape[:-1] + (weight.shape[1],))

def dense_back(grad_out, values_in, weight):
    grads_low = grad_out.astype(jnp.bfloat16).reshape(-1, grad_out.shape[-1])
    inputs_low = values_in.astype(jnp.bfloat16).reshape(-1, values_in.shape[-1])
    grad_in = jnp.dot(grads_low, weight.T, preferred_element_type=jnp.float32)
    grad_weight = jnp.dot(inputs_low.T, grads_low, preferred_element_type=jnp.float32)
    return (grad_in.reshape(values_in.shape), grad_weight)

def gelu_exact(values_in):
    return jax.nn.gelu(values_in, approximate=False)

def gelu_back(values_in, grad_out):
    return jax.vjp(gelu_exact, values_in)[1](grad_out)[0]

def depthwise(padded, kernel):
    channels = kernel.shape[1]
    taps = kernel.reshape(KS, KS, 1, channels)
    return lax.conv_general_dilated(padded, taps, (1, 1), 'VALID', dimension_numbers=('NHWC', 'HWIO', 'NHWC'), feature_group_count=channels, precision=lax.Precision.HIGHEST)

def flipped(kernel):
    channels = kernel.shape[1]
    return kernel.reshape(KS, KS, channels)[::-1, ::-1].reshape(KS * KS, channels)

def kernel_back(padded, kernel, grad_out):

    def apply_taps(argument):
        return depthwise(padded, argument)
    return jax.vjp(apply_taps, kernel)[1](grad_out)[0]

def pad_both(values_in):
    half = KS // 2
    return jnp.pad(values_in, ((0, 0), (half, half), (half, half), (0, 0)))

def patchify(pixels):
    number, channels, row_count, col_count = pixels.shape
    blocks = pixels.reshape(number, channels, row_count // PATCH, PATCH, col_count // PATCH, PATCH)
    return blocks.transpose(0, 2, 4, 1, 3, 5).reshape(number, row_count // PATCH, col_count // PATCH, channels * PATCH * PATCH)

def unpatchify(grads_in, channels):
    number, row_count, col_count, _ = grads_in.shape
    blocks = grads_in.reshape(number, row_count, col_count, channels, PATCH, PATCH)
    return blocks.transpose(0, 3, 1, 4, 2, 5).reshape(number, channels, row_count * PATCH, col_count * PATCH)

def merge_pairs(values_in):
    number, row_count, col_count, channels = values_in.shape
    blocks = values_in.reshape(number, row_count // 2, 2, col_count // 2, 2, channels)
    return blocks.transpose(0, 1, 3, 2, 4, 5).reshape(number, row_count // 2, col_count // 2, 4 * channels)

def split_pairs(grads_in, channels):
    number, row_count, col_count, _ = grads_in.shape
    blocks = grads_in.reshape(number, row_count, col_count, 2, 2, channels)
    return blocks.transpose(0, 1, 3, 2, 4, 5).reshape(number, row_count * 2, col_count * 2, channels)

def block_forward(inputs, padded, kernel, gain_vec, w_up, w_down, layer_scale):
    mixed_out = depthwise(padded, kernel)
    normed = norm_gain(mixed_out, gain_vec)
    upper_in = dense(normed, w_up)
    hidden = gelu_exact(upper_in)
    branch = dense(hidden, w_down)
    return (inputs + layer_scale * branch, (mixed_out, normed, upper_in, hidden))

def block_backward(grad_out, padded, kernel, gain_vec, w_up, w_down, layer_scale, stored):
    mixed_out, normed, upper_in, hidden = stored
    grad_branch = grad_out * layer_scale
    grad_hidden, grad_down = dense_back(grad_branch, hidden, w_down)
    grad_upper = gelu_back(upper_in, grad_hidden)
    grad_normed, grad_up = dense_back(grad_upper, normed, w_up)
    grad_mixed = norm_back(mixed_out, gain_vec, grad_normed)
    grad_kernel = kernel_back(padded, kernel, grad_mixed)
    return (grad_mixed, grad_kernel, grad_up, grad_down)

def section_two(held, labels, down_gain, ds_weight, head_gain, head_weight):
    source = held.astype(jnp.float32)
    normed_in = norm_gain(source, down_gain)
    merged = merge_pairs(normed_in)
    start_two = dense(merged, ds_weight)
    pooled = lax.optimization_barrier(jnp.mean(start_two, axis=(1, 2)))
    head_in = norm_gain(pooled, head_gain)
    logits = dense(head_in, head_weight)
    onehot = (labels[:, None] == lax.iota(jnp.int32, logits.shape[1])[None, :]).astype(jnp.float32)
    losses = jax.nn.logsumexp(logits, axis=1) - lax.optimization_barrier(jnp.sum(onehot * logits, axis=1))
    grad_logits = jax.nn.softmax(logits, axis=1) - onehot
    grad_head_in, grad_head = dense_back(grad_logits, head_in, head_weight)
    grad_pooled = norm_back(pooled, head_gain, grad_head_in)
    cells = start_two.shape[1] * start_two.shape[2]
    grad_start = jnp.broadcast_to((grad_pooled / cells)[:, None, None, :], start_two.shape)
    grad_merged, grad_ds = dense_back(grad_start, merged, ds_weight)
    grad_normed_in = split_pairs(grad_merged, source.shape[3])
    grad_source = norm_back(source, down_gain, grad_normed_in)
    grad_held = lax.optimization_barrier(grad_source.astype(jnp.bfloat16))
    return (losses, grad_held, (grad_ds, grad_head))

def reference(images, perturbation, labels, step_levels, stem_weight, stem_gain, dw1_kernel, norm1_gain, up1_weight, down1_weight, scale1, down_gain, ds_weight, head_gain, head_weight):
    kernel_one = dw1_kernel.astype(jnp.float32)

    def one_image(carry, item):
        image, label = item
        perturbed = image.astype(jnp.float32)[None] + perturbation[None]
        patches = patchify(perturbed)
        stem_pre = dense(patches, stem_weight)
        stem_out = lax.optimization_barrier(norm_gain(stem_pre, stem_gain).astype(jnp.bfloat16))
        padded_one = pad_both(stem_out).astype(jnp.float32)
        block_out, stored_one = block_forward(stem_out.astype(jnp.float32), padded_one, kernel_one, norm1_gain, up1_weight, down1_weight, scale1)
        section_out = lax.optimization_barrier(block_out.astype(jnp.bfloat16))
        losses, grad_held, grads_two = section_two(section_out, label[None], down_gain, ds_weight, head_gain, head_weight)
        grad_block = grad_held.astype(jnp.float32)
        grad_mixed, grad_dw1, grad_up1, grad_down1 = block_backward(grad_block, padded_one, kernel_one, norm1_gain, up1_weight, down1_weight, scale1, stored_one)
        grad_stem = grad_block + depthwise(pad_both(grad_mixed), flipped(kernel_one))
        grad_pre = norm_back(stem_pre, stem_gain, grad_stem)
        grad_patches, grad_stem_weight = dense_back(grad_pre, patches, stem_weight)
        grad_pixels = unpatchify(grad_patches, 3)[0]
        grad_ds, grad_head = grads_two
        terms = (grad_pixels, grad_stem_weight, grad_dw1, grad_up1, grad_down1, grad_ds, grad_head)
        return (tuple((held_sum + term for held_sum, term in zip(carry, terms))), losses[0])
    shapes = (perturbation.shape, stem_weight.shape, dw1_kernel.shape, up1_weight.shape, down1_weight.shape, ds_weight.shape, head_weight.shape)
    initial = tuple((jnp.zeros(shape_one, jnp.float32) for shape_one in shapes))
    carry, losses = lax.scan(one_image, initial, (images, labels))
    delta_grad = carry[0]
    spread = jnp.sqrt(jnp.mean(delta_grad * delta_grad) + EPS_ROOT)
    steps_size = STEP_UNIT * step_levels.astype(jnp.float32)[:, None, None]
    new_perturbation = jnp.clip(perturbation + steps_size * delta_grad / spread, -BOUND, BOUND)
    return (new_perturbation, losses, carry[1], carry[2], carry[3], carry[4], carry[5], carry[6])
```

```python
import jax
import jax.numpy as jnp
import numpy as np
from jax import lax
from jax.experimental import pallas as pl
from jax.experimental.pallas import tpu as pltpu
from jax.sharding import PartitionSpec as P

KS = 7
EPS_NORM = 1e-06
EPS_ROOT = 1e-12
BOUND = 0.5
STEP_UNIT = 0.1

NZ, NY, NXH, NXL, NC = 8, 4, 2, 2, 2
NX = NXH * NXL
ROWS, COLS, CELLS = 8, 32, 256
C1, F1, C2, CLASSES = 192, 768, 384, 62
WIDE = 256
PIECE = 48

F32 = jnp.float32
BF16 = jnp.bfloat16
MESH = pl.DeviceIdType.MESH


def index_table():
    table = np.full((8, F1), -1, np.int32)

    def owner(x_hi, y, z):
        return (z * NY + y) * NXH + x_hi

    for x_hi in range(NXH):
        for y in range(NY):
            for z in range(NZ):
                own = owner(x_hi, y, z)
                for q in range(6):
                    place = ((x_hi * NY + y) * NZ + z) * 6 + q
                    table[0, place] = own * 12 + q
                    table[0, 384 + place] = own * 12 + 6 + q
                    table[1, place] = own * 6 + q
                    if q < 3:
                        table[2, place] = own * 3 + q
                    else:
                        table[3, place] = own * 3 + q - 3
    for part_col in range(4):
        for strip in range(4):
            for channel in range(3):
                for row in range(8):
                    lane = part_col * 128 + strip * 24 + channel * 8 + row
                    table[4, lane] = channel * 16 + (row % 4) * 4 + part_col
                    table[5, lane] = strip * 2 + row // 4
    return table


def dot_nn(a, b):
    return lax.dot_general(a, b, (((1,), (0,)), ((), ())), preferred_element_type=F32)


def dot_nt(a, b):
    return lax.dot_general(a, b, (((1,), (1,)), ((), ())), preferred_element_type=F32)


def dot_tn(a, b):
    return lax.dot_general(a, b, (((0,), (0,)), ((), ())), preferred_element_type=F32)


def mean_lanes(values):
    return jnp.sum(values, axis=-1, keepdims=True) * (1.0 / values.shape[-1])


def norm_parts(values):
    centred = values - mean_lanes(values)
    root = lax.rsqrt(mean_lanes(centred * centred) + EPS_NORM)
    return centred * root, root


def norm_back(unit, root, grad):
    return root * (grad - mean_lanes(grad) - unit * mean_lanes(grad * unit))


def one_hot(index_row, rows):
    width = index_row.shape[1]
    return (lax.broadcasted_iota(jnp.int32, (rows, width), 0) == index_row).astype(F32).astype(BF16)


def first_row(values, rows=16):
    wide = jnp.broadcast_to(values[0:1], (rows, values.shape[1])).astype(F32)
    return jnp.where(lax.broadcasted_iota(jnp.int32, wide.shape, 0) == 0, wide, 0.0).astype(BF16)


def image_kernel(
    label,
    pixels,
    delta,
    table,
    stem_weight,
    stem_gain,
    taps,
    norm1_gain,
    up_weight,
    down_weight,
    scale1,
    down_gain,
    ds_weight,
    head_gain,
    head_weight,
    loss_out,
    first_out,
    second_out,
    delta_out,
    padded,
    shifted,
    mixed_ref,
    wide_ref,
    tap_grad,
    taps_ref,
):
    taps_ref[...] = taps[...].astype(F32)
    perturbed = (pixels[...].astype(F32) + delta[...]).reshape(96, 128)
    perturbed = jnp.concatenate([perturbed, jnp.zeros((32, 128), F32)], axis=0).astype(BF16)
    i0 = lax.broadcasted_iota(jnp.int32, (128, 128), 0)
    i1 = lax.broadcasted_iota(jnp.int32, (128, 128), 1)
    column_pick = (i1 == 4 * (i0 & 31) + (i0 >> 5)).astype(F32).astype(BF16)
    columns = dot_nt(column_pick, perturbed)
    columns = jnp.concatenate([columns[32 * k : 32 * k + 32] for k in range(4)], axis=1)
    row_of = table[5:6, 0:512]
    cells = jnp.concatenate(
        [jnp.where(row_of == r, columns, 0.0) for r in range(ROWS)], axis=0
    ).astype(BF16)
    feature_pick = one_hot(table[4:5, 0:512], 48)
    patches = dot_nt(cells, feature_pick).astype(BF16)

    stem_pre = dot_nn(patches, stem_weight[...])
    stem_unit, stem_root = norm_parts(stem_pre)
    stem_out = (stem_unit * stem_gain[...]).astype(BF16).astype(F32)

    def spread_columns(values):
        padded[:, 8 : 8 + COLS, :] = values.reshape(ROWS, COLS, C1)
        for j in range(KS):
            shifted[j] = padded[:, 5 + j : 5 + j + COLS, :]

    padded[:, 0:8, :] = jnp.zeros((ROWS, 8, C1), F32)
    padded[:, 8 + COLS :, :] = jnp.zeros((ROWS, 8, C1), F32)
    spread_columns(stem_out)
    for r in range(ROWS):
        total = None
        for i in range(KS):
            if 0 <= r + i - 3 < ROWS:
                for j in range(KS):
                    tap = KS * i + j
                    term = shifted[j, r + i - 3] * taps_ref[tap : tap + 1, :]
                    total = term if total is None else total + term
        mixed_ref[r] = total
    mixed = mixed_ref[...].reshape(CELLS, C1)

    mixed_unit, mixed_root = norm_parts(mixed)
    normed = (mixed_unit * norm1_gain[...]).astype(BF16)
    upper = dot_nn(normed, up_weight[...])
    half = 0.5 + 0.5 * lax.erf(upper * (0.5**0.5))
    hidden = (upper * half).astype(BF16)
    gelu_slope = half + upper * jnp.exp(-0.5 * upper * upper) * ((2.0 * np.pi) ** -0.5)
    branch = dot_nn(hidden, down_weight[...])
    section = (stem_out + scale1[...] * branch).astype(BF16).astype(F32)

    section_unit, section_root = norm_parts(section)
    merged = (section_unit * down_gain[...]).astype(BF16)
    p0 = lax.broadcasted_iota(jnp.int32, (16, CELLS), 0)
    p1 = lax.broadcasted_iota(jnp.int32, (16, CELLS), 1)
    place_pick = (p0 == 2 * ((p1 >> 5) & 1) + (p1 & 1)).astype(F32).astype(BF16)
    merged_sum = dot_nn(place_pick, merged)
    sums_high = merged_sum.astype(BF16)
    rest = merged_sum - sums_high.astype(F32)
    sums_mid = rest.astype(BF16)
    sums_low = (rest - sums_mid.astype(F32)).astype(BF16)
    row16 = lax.broadcasted_iota(jnp.int32, (16, C1), 0)

    def place_rows(place):
        high = sums_high[place : place + 1].astype(F32)
        mid = sums_mid[place : place + 1].astype(F32)
        low = sums_low[place : place + 1].astype(F32)
        return jnp.where(
            row16 == 0, high, jnp.where(row16 == 1, mid, jnp.where(row16 == 2, low, 0.0))
        ).astype(BF16)

    split_sums = [place_rows(place) for place in range(4)]
    pooled = None
    for place in range(4):
        term = dot_nn(split_sums[place], ds_weight[place * C1 : (place + 1) * C1, :])
        pooled = term if pooled is None else pooled + term
    cells_two = CELLS // 4
    pooled = jnp.sum(pooled, axis=0, keepdims=True) * (1.0 / cells_two)
    pooled = jnp.broadcast_to(pooled, (16, C2))
    head_unit, head_root = norm_parts(pooled)
    head_in = (head_unit * head_gain[...]).astype(BF16)
    logits = dot_nn(head_in, head_weight[...])
    onehot = (lax.broadcasted_iota(jnp.int32, logits.shape, 1) == label[0]).astype(F32)
    top = jnp.max(logits, axis=-1, keepdims=True)
    raised = jnp.exp(logits - top)
    mass = jnp.sum(raised, axis=-1, keepdims=True)
    losses = jnp.log(mass) + top - jnp.sum(onehot * logits, axis=-1, keepdims=True)
    loss_out[0] = losses[0, 0]
    grad_logits = (raised / mass - onehot).astype(BF16)
    grad_head_in = dot_nt(grad_logits, head_weight[...])
    grad_pooled = norm_back(head_unit, head_root, grad_head_in * head_gain[...])
    grad_start = (grad_pooled * (1.0 / cells_two)).astype(BF16)

    unit_pick = one_hot(table[1:2, 0:C2], C2)
    start_rows = dot_nn(grad_start, unit_pick).astype(BF16)
    wide_rows = lax.broadcasted_iota(jnp.int32, (16, C2), 0)
    start_rows = jnp.where(wide_rows < 3, start_rows.astype(F32), 0.0).astype(BF16)
    for place in range(4):
        grad_ds = dot_tn(start_rows, split_sums[place]).astype(BF16)
        for x_hi in range(NXH):
            for y in range(NY):
                at = (x_hi * NY + y) * PIECE
                block = grad_ds[at : at + PIECE]
                if place % 2 == 0:
                    first_out[2 + place // 2, x_hi, y, :, 0:C1] = block
                else:
                    second_out[2 + place // 2, y, x_hi, :, 0:C1] = block
    o0 = lax.broadcasted_iota(jnp.int32, (64, WIDE), 0)
    o1 = lax.broadcasted_iota(jnp.int32, (64, WIDE), 1)
    offset_pick = (o1 == o0 + C1).astype(F32).astype(BF16)
    grad_logits_wide = jnp.concatenate([grad_logits.astype(F32), jnp.zeros((16, 2), F32)], axis=1)
    placed_logits = first_row(dot_nn(grad_logits_wide.astype(BF16), offset_pick))
    head_rows = dot_nn(head_in, unit_pick).astype(BF16)
    grad_head = dot_tn(head_rows, placed_logits)

    place_grads = [
        dot_nt(grad_start, ds_weight[place * C1 : (place + 1) * C1, :])[0:1] * down_gain[...]
        for place in range(4)
    ]
    even = (lax.broadcasted_iota(jnp.int32, (COLS, C1), 0) & 1) == 0
    by_row = [
        jnp.where(even, place_grads[2 * k], place_grads[2 * k + 1]) for k in range(2)
    ]
    grad_unit = jnp.concatenate([by_row[r % 2] for r in range(ROWS)], axis=0)
    grad_block = norm_back(section_unit, section_root, grad_unit).astype(BF16).astype(F32)

    grad_branch = (grad_block * scale1[...]).astype(BF16)
    grad_hidden = dot_nt(grad_branch, down_weight[...])
    grad_upper = (grad_hidden * gelu_slope).astype(BF16)
    grad_normed = dot_nt(grad_upper, up_weight[...])
    grad_mixed = norm_back(mixed_unit, mixed_root, grad_normed * norm1_gain[...])

    hidden_pick = one_hot(table[0:1, :], F1)

    def store_rows(strip, grads, extra):
        for x_hi in range(NXH):
            for y in range(NY):
                at = (x_hi * NY + y) * PIECE
                block = grads[at : at + PIECE]
                if extra is not None:
                    block = block + extra[at : at + PIECE]
                first_out[strip, x_hi, y] = block.astype(BF16)
                second_out[strip, y, x_hi] = grads[384 + at : 384 + at + PIECE].astype(BF16)

    wide_ref[...] = jnp.zeros((CELLS, WIDE), BF16)
    wide_ref[:, 0:C1] = normed
    grad_up = dot_tn(dot_nn(grad_upper, hidden_pick).astype(BF16), wide_ref[...])
    store_rows(0, grad_up, grad_head)

    mixed_ref[...] = grad_mixed.reshape(ROWS, COLS, C1)
    tap_grad[...] = jnp.zeros_like(tap_grad)
    for i in range(KS):
        for j in range(KS):
            total = None
            for r in range(ROWS):
                if 0 <= r + i - 3 < ROWS:
                    term = shifted[j, r + i - 3] * mixed_ref[r]
                    total = term if total is None else total + term
            tap = KS * i + j
            tap_grad[tap : tap + 1, :] = jnp.sum(total, axis=0, keepdims=True)

    spread_columns(grad_mixed)
    for r in range(ROWS):
        total = None
        for i in range(KS):
            if 0 <= r + i - 3 < ROWS:
                for j in range(KS):
                    tap = KS * (KS - 1 - i) + (KS - 1 - j)
                    term = shifted[j, r + i - 3] * taps_ref[tap : tap + 1, :]
                    total = term if total is None else total + term
        mixed_ref[r] = total
    grad_stem = grad_block + mixed_ref[...].reshape(CELLS, C1)
    grad_pre = norm_back(stem_unit, stem_root, grad_stem * stem_gain[...]).astype(BF16)

    grad_stem_weight = dot_tn(patches, grad_pre)
    stem_rows = dot_nn(grad_stem_weight.astype(BF16), one_hot(table[2:3, 0:C2], C1))
    tap_rows = dot_nn(tap_grad[...].astype(BF16), one_hot(table[3:4, 0:C2], C1))
    stem_rows = jnp.concatenate([stem_rows, jnp.zeros((16, C2), F32)], axis=0)
    grad_small = dot_tn((stem_rows + tap_rows).astype(BF16), offset_pick)
    wide_ref[:, 0:C1] = grad_branch
    grad_down = dot_tn(dot_nn(hidden, hidden_pick).astype(BF16), wide_ref[...])
    store_rows(1, grad_down, grad_small)

    grad_patches = dot_nt(grad_pre, stem_weight[...]).astype(BF16)
    grad_cells = dot_nn(grad_patches, feature_pick)
    grad_columns = None
    for r in range(ROWS):
        term = jnp.where(row_of == r, grad_cells[r * COLS : (r + 1) * COLS], 0.0)
        grad_columns = term if grad_columns is None else grad_columns + term
    grad_columns = grad_columns.astype(BF16)
    grad_pixels = None
    for k in range(4):
        term = dot_tn(
            grad_columns[:, 128 * k : 128 * k + 128], column_pick[32 * k : 32 * k + 32, :]
        )
        grad_pixels = term if grad_pixels is None else grad_pixels + term
    delta_out[...] = grad_pixels[0:96].reshape(4, 24, 128)


def places():
    dp, strip = lax.axis_index("dp"), lax.axis_index("strip")
    z, y, x_hi = dp // (NY * NXH), (dp // NXH) % NY, dp % NXH
    x_lo, core = strip // NC, strip % NC
    return dp, strip, z, y, x_hi, x_lo, core


def exchange_kernel(images, strip_delta, pixels, delta, send, recv, local):
    dp, strip = lax.axis_index("dp"), lax.axis_index("strip")
    barrier = pltpu.get_barrier_semaphore()
    for t in range(1, 4):
        pl.semaphore_signal(barrier, inc=1, device_id=(dp, (strip + t) % 4), device_id_type=MESH)
    own = [
        pltpu.make_async_copy(images.at[strip], pixels.at[strip], local.at[0]),
        pltpu.make_async_copy(strip_delta, delta.at[strip], local.at[1]),
    ]
    for copy in own:
        copy.start()
    pl.semaphore_wait(barrier, 3)
    copies = []
    for t in range(1, 4):
        peer = (strip + t) % 4
        for k, (source, target) in enumerate(
            ((images.at[peer], pixels.at[strip]), (strip_delta, delta.at[strip]))
        ):
            copies.append(
                pltpu.make_async_remote_copy(
                    src_ref=source,
                    dst_ref=target,
                    send_sem=send.at[t - 1, k],
                    recv_sem=recv.at[t - 1, k],
                    device_id=(dp, peer),
                    device_id_type=MESH,
                )
            )
    for copy in copies:
        copy.start()
    for copy in own + copies:
        copy.wait()


def reduce_kernel(
    first,
    second,
    delta,
    shares,
    delta_sum,
    squares,
    core_a,
    core_b,
    core_p,
    held_a,
    held_b,
    held_p,
    got_a,
    got_b,
    got_p,
    next_a,
    next_b,
    next_p,
    last_a,
    last_b,
    last_p,
    rows_a,
    rows_b,
    stage,
    low,
    got_z,
    low_p,
    send,
    recv,
):
    dp, strip, z, y, x_hi, x_lo, core = places()
    x = x_hi * NXL + x_lo

    def x_peer(t):
        other = (x + t) % NX
        other_hi, other_lo = other // NXL, other % NXL
        return other_hi, other_lo, ((z * NY + y) * NXH + other_hi, other_lo * NC + core)

    def y_peer(t):
        other = (y + t) % NY
        return other, ((z * NY + other) * NXH + x_hi, strip)

    def z_peer(t):
        other = (z + t) % NZ
        return other, ((other * NY + y) * NXH + x_hi, strip)

    def strip_peer(t):
        return (dp, (strip + t) % (NXL * NC))

    barrier = pltpu.get_barrier_semaphore()
    peers = [x_peer(t)[2] for t in range(1, NX)] + [y_peer(t)[1] for t in range(1, NY)]
    peers += [z_peer(t)[1] for t in range(1, NZ)] + [strip_peer(t) for t in range(1, 4)]
    for peer in peers:
        pl.semaphore_signal(barrier, inc=1, device_id=peer, device_id_type=MESH)
    pl.semaphore_wait(barrier, len(peers))

    count = [0]

    def ship(source, target, peer):
        k = count[0]
        count[0] += 1
        copy = pltpu.make_async_remote_copy(
            src_ref=source,
            dst_ref=target,
            send_sem=send.at[k],
            recv_sem=recv.at[k],
            device_id=peer,
            device_id_type=MESH,
        )
        copy.start()
        return copy

    def settle(copies):
        for copy in copies:
            copy.wait()

    partner = (dp, x_lo * NC + (1 - core))
    sent = []
    for lo in range(NXL):
        theirs = lo * NC + (1 - core)
        sent.append(ship(first.at[theirs], core_a.at[lo], partner))
        sent.append(ship(second.at[theirs], core_b.at[lo], partner))
        sent.append(ship(delta.at[theirs], core_p.at[lo], partner))
    settle(sent)
    for lo in range(NXL):
        mine = lo * NC + core
        held_a[lo] = (first[mine].astype(F32) + core_a[lo].astype(F32)).astype(BF16)
        for k in range(NY):
            held_b[k, lo] = (second[mine, k].astype(F32) + core_b[lo, k].astype(F32)).astype(BF16)
        held_p[lo] = delta[mine] + core_p[lo]

    sent = []
    for t in range(1, 4):
        other_hi, other_lo, peer = x_peer(t)
        sent.append(ship(held_a.at[other_lo, other_hi], got_a.at[t - 1], peer))
        sent.append(ship(held_p.at[other_lo], got_p.at[x], peer))
        other, peer = y_peer(t)
        sent.append(ship(held_b.at[other], got_b.at[t - 1], peer))
    got_p[x] = held_p[x_lo]
    settle(sent)
    total = held_a[x_lo, x_hi].astype(F32)
    for t in range(3):
        total = total + got_a[t].astype(F32)
    next_a[...] = total.astype(BF16)
    total = held_b[y].astype(F32)
    for t in range(3):
        total = total + got_b[t].astype(F32)
    next_b[...] = total.astype(BF16)
    next_p[...] = (got_p[0] + got_p[1]) + (got_p[2] + got_p[3])

    sent = []
    for t in range(1, 4):
        other, peer = y_peer(t)
        sent.append(ship(next_a.at[other], last_a.at[t - 1], peer))
        sent.append(ship(next_p, last_p.at[y], peer))
        other_hi, other_lo, peer = x_peer(t)
        sent.append(ship(next_b.at[other_lo, other_hi], last_b.at[t - 1], peer))
    last_p[y] = next_p[...]
    settle(sent)
    total = next_a[y].astype(F32)
    for t in range(3):
        total = total + last_a[t].astype(F32)
    rows_a[...] = total
    total = next_b[x_lo, x_hi].astype(F32)
    for t in range(3):
        total = total + last_b[t].astype(F32)
    rows_b[...] = total
    low_p[z] = ((last_p[0] + last_p[1]) + (last_p[2] + last_p[3])).astype(BF16)
    for k in range(NZ):
        stage[k, 12:16] = jnp.zeros((4, WIDE), F32)
        stage[k, 0:6] = rows_a[6 * k : 6 * k + 6]
        stage[k, 6:12] = rows_b[6 * k : 6 * k + 6]
    low[...] = stage[...].astype(BF16)

    sent = []
    for t in range(1, NZ):
        other, peer = z_peer(t)
        sent.append(ship(low.at[other], got_z.at[t - 1], peer))
        sent.append(ship(low_p.at[z], low_p.at[z], peer))
    settle(sent)
    total = stage[z]
    for t in range(NZ - 1):
        total = total + got_z[t].astype(F32)
    shares[strip] = total
    total = low_p[0].astype(F32)
    for k in range(1, NZ):
        total = total + low_p[k].astype(F32)
    delta_sum[...] = total
    square = total * total
    squares[strip] = square[0:8] + square[8:16] + square[16:24]

    sent = []
    for t in range(1, 4):
        peer = strip_peer(t)
        sent.append(ship(shares.at[strip], shares.at[strip], peer))
        sent.append(ship(squares.at[strip], squares.at[strip], peer))
    settle(sent)


N_COPIES = 6 + 9 + 9 + 14 + 6


def finish_kernel(
    levels,
    shares,
    delta_sum,
    squares,
    perturbation,
    new_out,
    stem_out,
    dw_out,
    up_out,
    down_out,
    ds_out,
    head_out,
):
    total = jnp.sum((squares[0] + squares[1]) + (squares[2] + squares[3]))
    spread = jnp.sqrt(jnp.full((8, 128), total, F32) * (1.0 / 12288) + EPS_ROOT)
    for channel in range(3):
        level = STEP_UNIT * levels[channel].astype(F32)
        step = level * delta_sum[8 * channel : 8 * channel + 8] / spread
        new_out[channel] = jnp.clip(perturbation[channel] + step, -BOUND, BOUND)
    up_out[...] = shares[0].T[0:C1, 0:12]
    down_out[...] = shares[1][0:12, 0:C1]
    for k in range(2):
        turned = shares[2 + k].T
        for half in range(2):
            place = 2 * k + half
            ds_out[place * C1 : (place + 1) * C1, :] = turned[0:C1, 6 * half : 6 * half + 6]
    head_out[...] = shares[0][0:6, C1 : C1 + CLASSES]
    turned = shares[1].T
    stem_out[...] = turned[C1 : C1 + 48, 0:3]
    dw_out[...] = turned[C1 : C1 + 49, 3:6]


VMEM = pl.BlockSpec(memory_space=pltpu.VMEM)
SMEM = pl.BlockSpec(memory_space=pltpu.SMEM)


def shaped(shape, dtype):
    return jax.ShapeDtypeStruct(shape, dtype)


def run_exchange(images, perturbation):
    return pl.pallas_call(
        exchange_kernel,
        name="strip_exchange",
        out_shape=(shaped((4, 3, 8, 128), BF16), shaped((4, 3, 8, 128), F32)),
        in_specs=[VMEM] * 2,
        out_specs=(VMEM, VMEM),
        scratch_shapes=[
            pltpu.SemaphoreType.DMA((3, 2)),
            pltpu.SemaphoreType.DMA((3, 2)),
            pltpu.SemaphoreType.DMA((2,)),
        ],
        compiler_params=pltpu.CompilerParams(collective_id=0, has_side_effects=True),
    )(images, perturbation)


def run_image(labels, *operands):
    return pl.pallas_call(
        image_kernel,
        name="image_step",
        out_shape=(
            shaped((1,), F32),
            shaped((4, NXH, NY, PIECE, WIDE), BF16),
            shaped((4, NY, NXH, PIECE, WIDE), BF16),
            shaped((4, 24, 128), F32),
        ),
        in_specs=[SMEM] + [VMEM] * len(operands),
        out_specs=(SMEM, VMEM, VMEM, VMEM),
        scratch_shapes=[
            pltpu.VMEM((ROWS, COLS + 16, C1), F32),
            pltpu.VMEM((KS, ROWS, COLS, C1), F32),
            pltpu.VMEM((ROWS, COLS, C1), F32),
            pltpu.VMEM((CELLS, WIDE), BF16),
            pltpu.VMEM((64, C1), F32),
            pltpu.VMEM((KS * KS, C1), F32),
        ],
        compiler_params=pltpu.CompilerParams(vmem_limit_bytes=48 * 1024 * 1024),
    )(labels, *operands)


def run_reduce(first, second, delta):
    half_a = (NXL, NXH, NY, PIECE, WIDE)
    return pl.pallas_call(
        reduce_kernel,
        name="grad_reduce",
        out_shape=(
            shaped((4, 16, WIDE), F32),
            shaped((24, 128), F32),
            shaped((4, 8, 128), F32),
        ),
        in_specs=[VMEM] * 3,
        out_specs=(VMEM,) * 3,
        scratch_shapes=[
            pltpu.VMEM(half_a, BF16),
            pltpu.VMEM((NXL, NY, NXH, PIECE, WIDE), BF16),
            pltpu.VMEM((NXL, 24, 128), F32),
            pltpu.VMEM(half_a, BF16),
            pltpu.VMEM((NY, NXL, NXH, PIECE, WIDE), BF16),
            pltpu.VMEM((NXL, 24, 128), F32),
            pltpu.VMEM((3, NY, PIECE, WIDE), BF16),
            pltpu.VMEM((3, NXL, NXH, PIECE, WIDE), BF16),
            pltpu.VMEM((NX, 24, 128), F32),
            pltpu.VMEM((NY, PIECE, WIDE), BF16),
            pltpu.VMEM((NXL, NXH, PIECE, WIDE), BF16),
            pltpu.VMEM((24, 128), F32),
            pltpu.VMEM((3, PIECE, WIDE), BF16),
            pltpu.VMEM((3, PIECE, WIDE), BF16),
            pltpu.VMEM((NY, 24, 128), F32),
            pltpu.VMEM((PIECE, WIDE), F32),
            pltpu.VMEM((PIECE, WIDE), F32),
            pltpu.VMEM((NZ, 16, WIDE), F32),
            pltpu.VMEM((NZ, 16, WIDE), BF16),
            pltpu.VMEM((NZ - 1, 16, WIDE), BF16),
            pltpu.VMEM((NZ, 24, 128), BF16),
            pltpu.SemaphoreType.DMA((N_COPIES,)),
            pltpu.SemaphoreType.DMA((N_COPIES,)),
        ],
        compiler_params=pltpu.CompilerParams(collective_id=1, has_side_effects=True),
    )(first, second, delta)


def run_finish(levels, shares, delta_sum, squares, perturbation):
    return pl.pallas_call(
        finish_kernel,
        name="finish",
        out_shape=(
            shaped((3, 8, 128), F32),
            shaped((48, 3), F32),
            shaped((49, 3), F32),
            shaped((C1, 12), F32),
            shaped((12, C1), F32),
            shaped((4 * C1, 6), F32),
            shaped((6, CLASSES), F32),
        ),
        in_specs=[SMEM] + [VMEM] * 4,
        out_specs=(VMEM,) * 7,
    )(levels, shares, delta_sum, squares, perturbation)


def on_device(
    images,
    perturbation,
    labels,
    step_levels,
    stem_weight,
    stem_gain,
    dw1_kernel,
    norm1_gain,
    up1_weight,
    down1_weight,
    scale1,
    down_gain,
    ds_weight,
    head_gain,
    head_weight,
):
    pixels, delta = run_exchange(images, perturbation)
    table = jnp.asarray(index_table())
    loss, first, second, delta_grad = run_image(
        labels,
        pixels,
        delta,
        table,
        stem_weight,
        stem_gain.reshape(1, C1),
        dw1_kernel,
        norm1_gain.reshape(1, C1),
        up1_weight,
        down1_weight,
        scale1.reshape(1, C1),
        down_gain.reshape(1, C1),
        ds_weight,
        head_gain.reshape(1, C2),
        head_weight,
    )
    shares, delta_sum, squares = run_reduce(first, second, delta_grad)
    new_delta, stem, dw, up, down, ds, head = run_finish(
        step_levels, shares, delta_sum, squares, perturbation
    )
    return (new_delta, loss, stem, dw, up, down, ds, head)


def solution(mesh):
    return jax.shard_map(
        on_device,
        mesh=mesh,
        in_specs=(
            P("dp", None, "strip", None),
            P(None, "strip", None),
            P(("dp", "strip")),
        )
        + (P(),) * 12,
        out_specs=(
            P(None, "strip", None),
            P(("dp", "strip")),
            P(None, "dp"),
            P(None, "dp"),
            P(None, "dp"),
            P("dp", None),
            P(None, "dp"),
            P("dp", None),
        ),
        check_vma=False,
    )
```

```python
import jax
import jax.numpy as jnp
import numpy as np
from jax import lax
from jax.experimental import pallas as pl
from jax.experimental.pallas import tpu as pltpu
from jax.sharding import PartitionSpec as P

KS = 7
EPS_NORM = 1e-06
EPS_ROOT = 1e-12
BOUND = 0.5
STEP_UNIT = 0.1

NZ, NY, NXH, NXL, NC = 8, 4, 2, 2, 2
NX = NXH * NXL
ROWS, COLS, CELLS = 8, 32, 256
C1, F1, C2, CLASSES = 192, 768, 384, 62
WIDE = 256
PIECE = 48

F32 = jnp.float32
BF16 = jnp.bfloat16
MESH = pl.DeviceIdType.MESH


def index_table():
    table = np.full((8, F1), -1, np.int32)
    slots = {(0, 0): (2, 0), (0, 1): (6, 1), (1, 0): (2, 2), (1, 1): (7, 0), (2, 0): (3, 1), (2, 1): (7, 2)}
    for x_hi in range(NXH):
        for y in range(NY):
            for z in range(NZ):
                own = (z * NY + y) * NXH + x_hi
                block = (x_hi * NY + y) * NZ + z
                for q in range(6):
                    table[0, 6 * block + q] = own * 12 + q
                    table[0, 384 + 6 * block + q] = own * 12 + 6 + q
                    table[1, 6 * block + q] = own * 6 + q
                for (strip, _), (row, column) in slots.items():
                    table[row, strip * 64 + block] = own * 3 + column
    for part_col in range(4):
        for strip in range(4):
            for channel in range(3):
                for row in range(8):
                    lane = part_col * 128 + strip * 24 + channel * 8 + row
                    table[4, lane] = channel * 16 + (row % 4) * 4 + part_col
                    table[5, lane] = strip * 2 + row // 4
    return table


def dot_nn(a, b):
    return lax.dot_general(a, b, (((1,), (0,)), ((), ())), preferred_element_type=F32)


def dot_nt(a, b):
    return lax.dot_general(a, b, (((1,), (1,)), ((), ())), preferred_element_type=F32)


def dot_tn(a, b):
    return lax.dot_general(a, b, (((0,), (0,)), ((), ())), preferred_element_type=F32)


def mean_lanes(values):
    return jnp.sum(values, axis=-1, keepdims=True) * (1.0 / values.shape[-1])


def norm_parts(values):
    centred = values - mean_lanes(values)
    root = lax.rsqrt(mean_lanes(centred * centred) + EPS_NORM)
    return centred * root, root


def norm_back(unit, root, grad):
    return root * (grad - mean_lanes(grad) - unit * mean_lanes(grad * unit))


def one_hot(index_row, rows):
    width = index_row.shape[1]
    return (lax.broadcasted_iota(jnp.int32, (rows, width), 0) == index_row).astype(F32).astype(BF16)


def first_row(values, rows=16):
    wide = jnp.broadcast_to(values[0:1], (rows, values.shape[1])).astype(F32)
    return jnp.where(lax.broadcasted_iota(jnp.int32, wide.shape, 0) == 0, wide, 0.0).astype(BF16)


def step_kernel(
    label,
    head_gain,
    images,
    strip_delta,
    table_in,
    stem_in,
    stem_gain_in,
    taps_in,
    norm1_in,
    up_in,
    down_in,
    scale_in,
    down_gain_in,
    ds_in,
    head_in_t,
    shares,
    misc,
    pixels,
    delta,
    table,
    stem_weight,
    stem_gain,
    taps,
    norm1_gain,
    up_weight,
    down_weight,
    scale1,
    down_gain,
    ds_weight,
    head_weight,
    padded,
    shifted,
    mixed_ref,
    wide_merged,
    wide_normed,
    wide_branch,
    tap_grad,
    taps_ref,
    hidden_pick,
    unit_pick,
    ds_lo,
    ds_hi,
    ud_lo,
    ud_hi,
    small,
    delta_grad,
    c_ds_lo,
    c_ds_hi,
    c_ud_lo,
    c_ud_hi,
    c_small,
    c_delta,
    h_ds_lo,
    h_ds_hi,
    h_ud_lo,
    h_ud_hi,
    h_small,
    h_delta,
    x_ds_lo,
    x_ds_hi,
    x_ud_lo,
    x_ud_hi,
    x_small,
    x_delta,
    n_ds_lo,
    n_ds_hi,
    n_ud_lo,
    n_ud_hi,
    n_small,
    n_delta,
    y_ds_lo,
    y_ds_hi,
    y_ud_lo,
    y_ud_hi,
    y_small,
    y_delta,
    rows_ds,
    rows_ud,
    rows_small,
    stage,
    low,
    got_z,
    low_delta,
    local,
    send,
    recv,
):
    dp, strip = lax.axis_index("dp"), lax.axis_index("strip")
    z, y, x_hi = dp // (NY * NXH), (dp // NXH) % NY, dp % NXH
    x_lo, core = strip // NC, strip % NC
    x = x_hi * NXL + x_lo

    def x_peer(t):
        other = (x + t) % NX
        other_hi, other_lo = other // NXL, other % NXL
        return other_hi, other_lo, ((z * NY + y) * NXH + other_hi, other_lo * NC + core)

    def y_peer(t):
        other = (y + t) % NY
        return other, ((z * NY + other) * NXH + x_hi, strip)

    def z_peer(t):
        other = (z + t) % NZ
        return other, ((other * NY + y) * NXH + x_hi, strip)

    def strip_peer(t):
        return (strip + t) % (NXL * NC)

    barrier = pltpu.get_barrier_semaphore()
    peers = [(dp, strip_peer(t)) for t in range(1, 4)]
    peers += [x_peer(t)[2] for t in range(1, NX)] + [y_peer(t)[1] for t in range(1, NY)]
    peers += [z_peer(t)[1] for t in range(1, NZ)]
    for peer in peers:
        pl.semaphore_signal(barrier, inc=1, device_id=peer, device_id_type=MESH)

    loads = {}
    for k, (name, source, target) in enumerate(
        (
            ("table", table_in, table),
            ("pixels", images.at[strip], pixels.at[strip]),
            ("delta", strip_delta, delta.at[strip]),
            ("stem", stem_in, stem_weight),
            ("stem_gain", stem_gain_in, stem_gain),
            ("taps", taps_in, taps),
            ("norm1", norm1_in, norm1_gain),
            ("up", up_in, up_weight),
            ("down", down_in, down_weight),
            ("scale", scale_in, scale1),
            ("down_gain", down_gain_in, down_gain),
            ("ds", ds_in, ds_weight),
            ("head", head_in_t, head_weight),
        )
    ):
        loads[name] = pltpu.make_async_copy(source, target, local.at[k])
        loads[name].start()

    count = [0]

    def ship(source, target, peer):
        k = count[0]
        count[0] += 1
        copy = pltpu.make_async_remote_copy(
            src_ref=source,
            dst_ref=target,
            send_sem=send.at[k],
            recv_sem=recv.at[k],
            device_id=peer,
            device_id_type=MESH,
        )
        copy.start()
        return copy

    def settle(copies):
        for copy in copies:
            copy.wait()

    wide_merged[...] = jnp.zeros((CELLS, WIDE), BF16)
    wide_normed[...] = jnp.zeros((CELLS, WIDE), BF16)
    wide_branch[...] = jnp.zeros((CELLS, WIDE), BF16)
    tap_grad[...] = jnp.zeros_like(tap_grad)
    padded[:, 0:8, :] = jnp.zeros((ROWS, 8, C1), F32)
    padded[:, 8 + COLS :, :] = jnp.zeros((ROWS, 8, C1), F32)
    loads["table"].wait()
    hidden_pick[...] = one_hot(table[0:1, :], F1)
    unit_pick[...] = one_hot(table[1:2, 0:C2], C2)
    loads["taps"].wait()
    taps_ref[...] = taps[...].astype(F32)
    pl.semaphore_wait(barrier, len(peers))

    sent = []
    for t in range(1, 4):
        peer = strip_peer(t)
        sent.append(ship(images.at[peer], pixels.at[strip], (dp, peer)))
        sent.append(ship(strip_delta, delta.at[strip], (dp, peer)))
    for name in (
        "pixels", "delta", "stem", "stem_gain", "norm1", "up", "down", "scale", "down_gain", "ds", "head"
    ):
        loads[name].wait()
    settle(sent)

    perturbed = (pixels[...].astype(F32) + delta[...]).reshape(96, 128)
    perturbed = jnp.concatenate([perturbed, jnp.zeros((32, 128), F32)], axis=0).astype(BF16)
    i0 = lax.broadcasted_iota(jnp.int32, (128, 128), 0)
    i1 = lax.broadcasted_iota(jnp.int32, (128, 128), 1)
    column_pick = (i1 == 4 * (i0 & 31) + (i0 >> 5)).astype(F32).astype(BF16)
    columns = dot_nt(column_pick, perturbed)
    columns = jnp.concatenate([columns[32 * k : 32 * k + 32] for k in range(4)], axis=1)
    row_of = table[5:6, 0:512]
    cells = jnp.concatenate(
        [jnp.where(row_of == r, columns, 0.0) for r in range(ROWS)], axis=0
    ).astype(BF16)
    feature_pick = one_hot(table[4:5, 0:512], 48)
    patches = dot_nt(cells, feature_pick).astype(BF16)

    stem_pre = dot_nn(patches, stem_weight[...])
    stem_unit, stem_root = norm_parts(stem_pre)
    stem_out = (stem_unit * stem_gain[...]).astype(BF16).astype(F32)

    def spread_columns(values):
        padded[:, 8 : 8 + COLS, :] = values.reshape(ROWS, COLS, C1)
        for j in range(KS):
            shifted[j] = padded[:, 5 + j : 5 + j + COLS, :]

    def correlate(tap_of):
        for r in range(ROWS):
            total = None
            for i in range(KS):
                if 0 <= r + i - 3 < ROWS:
                    for j in range(KS):
                        tap = tap_of(i, j)
                        term = shifted[j, r + i - 3] * taps_ref[tap : tap + 1, :]
                        total = term if total is None else total + term
            mixed_ref[r] = total
        return mixed_ref[...].reshape(CELLS, C1)

    spread_columns(stem_out)
    mixed = correlate(lambda i, j: KS * i + j)

    mixed_unit, mixed_root = norm_parts(mixed)
    normed = (mixed_unit * norm1_gain[...]).astype(BF16)
    wide_normed[:, 0:C1] = normed
    upper = dot_nn(normed, up_weight[...])
    half = 0.5 + 0.5 * lax.erf(upper * (0.5**0.5))
    hidden = (upper * half).astype(BF16)
    gelu_slope = half + upper * jnp.exp(-0.5 * upper * upper) * ((2.0 * np.pi) ** -0.5)
    branch = dot_nt(hidden, down_weight[...])
    section = (stem_out + scale1[...] * branch).astype(BF16).astype(F32)

    section_unit, section_root = norm_parts(section)
    wide_merged[:, 0:C1] = (section_unit * down_gain[...]).astype(BF16)
    p0 = lax.broadcasted_iota(jnp.int32, (16, CELLS), 0)
    p1 = lax.broadcasted_iota(jnp.int32, (16, CELLS), 1)
    place_pick = (p0 == 2 * ((p1 >> 5) & 1) + (p1 & 1)).astype(F32).astype(BF16)
    merged_sum = dot_nn(place_pick, wide_merged[...])
    sums_high = merged_sum.astype(BF16).astype(F32)
    rest = merged_sum - sums_high
    sums_mid = rest.astype(BF16).astype(F32)
    sums_low = rest - sums_mid
    row16 = lax.broadcasted_iota(jnp.int32, (16, WIDE), 0)

    def place_rows(place):
        high = sums_high[place : place + 1]
        mid = sums_mid[place : place + 1]
        lowest = sums_low[place : place + 1]
        return jnp.where(
            row16 == 0, high, jnp.where(row16 == 1, mid, jnp.where(row16 == 2, lowest, 0.0))
        ).astype(BF16)

    split_sums = [place_rows(place) for place in range(4)]
    pooled = None
    for place in range(4):
        term = dot_nn(split_sums[place][:, 0:C1], ds_weight[place * C1 : (place + 1) * C1, :])
        pooled = term if pooled is None else pooled + term
    cells_two = CELLS // 4
    pooled = jnp.sum(pooled, axis=0, keepdims=True) * (1.0 / cells_two)
    pooled = jnp.broadcast_to(pooled, (16, C2))
    head_unit, head_root = norm_parts(pooled)
    gain = head_gain[...].reshape(1, C2)
    head_in = (head_unit * gain).astype(BF16)
    logits = dot_nt(head_in, head_weight[...])
    onehot = (lax.broadcasted_iota(jnp.int32, logits.shape, 1) == label[0]).astype(F32)
    top = jnp.max(logits, axis=-1, keepdims=True)
    raised = jnp.exp(logits - top)
    mass = jnp.sum(raised, axis=-1, keepdims=True)
    losses = jnp.log(mass) + top - jnp.sum(onehot * logits, axis=-1, keepdims=True)
    misc[3] = jnp.broadcast_to(losses[0:8], (8, 128))
    grad_logits = (raised / mass - onehot).astype(BF16)
    grad_head_in = dot_nn(grad_logits, head_weight[...])
    grad_pooled = norm_back(head_unit, head_root, grad_head_in * gain)
    grad_start = (grad_pooled * (1.0 / cells_two)).astype(BF16)

    def store_rows(first, second, at_strip, grads):
        for hi in range(NXH):
            for k in range(NY):
                at = (hi * NY + k) * PIECE
                block = grads[at : at + PIECE].astype(BF16)
                first[at_strip, hi, k] = block[:, 0:128]
                second[at_strip, k, hi] = block[:, 128:256]

    start_rows = dot_nn(grad_start, unit_pick[...])
    wide_rows = lax.broadcasted_iota(jnp.int32, (16, C2), 0)
    start_rows = jnp.where(wide_rows < 3, start_rows, 0.0).astype(BF16)
    o0 = lax.broadcasted_iota(jnp.int32, (64, WIDE), 0)
    o1 = lax.broadcasted_iota(jnp.int32, (64, WIDE), 1)
    head_offset = (o1 == o0 + C1).astype(F32).astype(BF16)
    grad_logits_wide = jnp.concatenate([grad_logits.astype(F32), jnp.zeros((16, 2), F32)], axis=1)
    placed_logits = first_row(dot_nn(grad_logits_wide.astype(BF16), head_offset))
    head_rows = dot_nn(head_in, unit_pick[...]).astype(BF16)
    for place in range(4):
        grad_ds = dot_tn(start_rows, split_sums[place])
        if place == 0:
            grad_ds = grad_ds + dot_tn(head_rows, placed_logits)
        store_rows(ds_lo, ds_hi, place, grad_ds)

    def core_start(*pairs):
        copies = []
        partner = (dp, x_lo * NC + (1 - core))
        for lo in range(NXL):
            for source, target in pairs:
                copies.append(ship(source.at[lo * NC + (1 - core)], target.at[lo], partner))
        return copies

    def core_sum(own_lo, own_hi, got_lo, got_hi, held_lo, held_hi):
        for lo in range(NXL):
            mine = lo * NC + core
            held_lo[lo] = (own_lo[mine].astype(F32) + got_lo[lo].astype(F32)).astype(BF16)
            for k in range(NY):
                block = own_hi[mine, k].astype(F32) + got_hi[lo, k].astype(F32)
                held_hi[k, lo] = block.astype(BF16)

    def first_start(held_lo, held_hi, got_lo, got_hi):
        copies = []
        for t in range(1, 4):
            other_hi, other_lo, peer = x_peer(t)
            copies.append(ship(held_lo.at[other_lo, other_hi], got_lo.at[t - 1], peer))
            other, peer = y_peer(t)
            copies.append(ship(held_hi.at[other], got_hi.at[t - 1], peer))
        return copies

    def first_sum(held_lo, held_hi, got_lo, got_hi, next_lo, next_hi):
        total = held_lo[x_lo, x_hi].astype(F32)
        for t in range(3):
            total = total + got_lo[t].astype(F32)
        next_lo[...] = total.astype(BF16)
        total = held_hi[y].astype(F32)
        for t in range(3):
            total = total + got_hi[t].astype(F32)
        next_hi[...] = total.astype(BF16)

    def second_start(next_lo, next_hi, got_lo, got_hi):
        copies = []
        for t in range(1, 4):
            other, peer = y_peer(t)
            copies.append(ship(next_lo.at[other], got_lo.at[t - 1], peer))
            other_hi, other_lo, peer = x_peer(t)
            copies.append(ship(next_hi.at[other_lo, other_hi], got_hi.at[t - 1], peer))
        return copies

    def second_sum(next_lo, next_hi, got_lo, got_hi, rows):
        total = next_lo[y].astype(F32)
        for t in range(3):
            total = total + got_lo[t].astype(F32)
        rows[:, 0:128] = total
        total = next_hi[x_lo, x_hi].astype(F32)
        for t in range(3):
            total = total + got_hi[t].astype(F32)
        rows[:, 128:256] = total

    core_ds = core_start((ds_lo, c_ds_lo), (ds_hi, c_ds_hi))

    place_grads = [
        dot_nt(grad_start, ds_weight[place * C1 : (place + 1) * C1, :])[0:1] * down_gain[...]
        for place in range(4)
    ]
    even = (lax.broadcasted_iota(jnp.int32, (COLS, C1), 0) & 1) == 0
    by_row = [
        jnp.where(even, place_grads[2 * k], place_grads[2 * k + 1]) for k in range(2)
    ]
    grad_unit = jnp.concatenate([by_row[r % 2] for r in range(ROWS)], axis=0)
    grad_block = norm_back(section_unit, section_root, grad_unit).astype(BF16).astype(F32)

    grad_branch = (grad_block * scale1[...]).astype(BF16)
    wide_branch[:, 0:C1] = grad_branch
    grad_down = dot_tn(dot_nn(hidden, hidden_pick[...]).astype(BF16), wide_branch[...])
    store_rows(ud_lo, ud_hi, 2, grad_down[0:384])
    store_rows(ud_lo, ud_hi, 3, grad_down[384:768])
    grad_hidden = dot_nn(grad_branch, down_weight[...])
    grad_upper = (grad_hidden * gelu_slope).astype(BF16)
    grad_up = dot_tn(dot_nn(grad_upper, hidden_pick[...]).astype(BF16), wide_normed[...])
    store_rows(ud_lo, ud_hi, 0, grad_up[0:384])
    store_rows(ud_lo, ud_hi, 1, grad_up[384:768])
    core_ud = core_start((ud_lo, c_ud_lo), (ud_hi, c_ud_hi))

    settle(core_ds)
    core_sum(ds_lo, ds_hi, c_ds_lo, c_ds_hi, h_ds_lo, h_ds_hi)
    first_ds = first_start(h_ds_lo, h_ds_hi, x_ds_lo, x_ds_hi)

    grad_normed = dot_nt(grad_upper, up_weight[...])
    grad_mixed = norm_back(mixed_unit, mixed_root, grad_normed * norm1_gain[...])

    mixed_ref[...] = grad_mixed.reshape(ROWS, COLS, C1)
    for i in range(KS):
        for j in range(KS):
            total = None
            for r in range(ROWS):
                if 0 <= r + i - 3 < ROWS:
                    term = shifted[j, r + i - 3] * mixed_ref[r]
                    total = term if total is None else total + term
            tap = KS * i + j
            tap_grad[tap : tap + 1, :] = jnp.sum(total, axis=0, keepdims=True)

    settle(core_ud)
    core_sum(ud_lo, ud_hi, c_ud_lo, c_ud_hi, h_ud_lo, h_ud_hi)
    first_ud = first_start(h_ud_lo, h_ud_hi, x_ud_lo, x_ud_hi)

    spread_columns(grad_mixed)
    grad_stem = grad_block + correlate(lambda i, j: KS * (KS - 1 - i) + (KS - 1 - j))
    grad_pre = norm_back(stem_unit, stem_root, grad_stem * stem_gain[...]).astype(BF16)

    grad_patches = dot_nt(grad_pre, stem_weight[...]).astype(BF16)
    grad_cells = dot_nn(grad_patches, feature_pick)
    grad_columns = None
    for r in range(ROWS):
        term = jnp.where(row_of == r, grad_cells[r * COLS : (r + 1) * COLS], 0.0)
        grad_columns = term if grad_columns is None else grad_columns + term
    grad_columns = grad_columns.astype(BF16)
    grad_pixels = None
    for k in range(4):
        term = dot_tn(
            grad_columns[:, 128 * k : 128 * k + 128], column_pick[32 * k : 32 * k + 32, :]
        )
        grad_pixels = term if grad_pixels is None else grad_pixels + term
    delta_grad[...] = grad_pixels[0:96].reshape(4, 24, 128)

    stem_low = dot_tn(patches, grad_pre)
    stem_low = jnp.concatenate([stem_low, jnp.zeros((16, C1), F32)], axis=0).astype(BF16)
    tap_low = tap_grad[...].astype(BF16)
    slots = []
    for stem_at, tap_at in ((2, 3), (6, 7)):
        slot = dot_nn(stem_low, one_hot(table[stem_at : stem_at + 1, 0:256], C1))
        slot = slot + dot_nn(tap_low, one_hot(table[tap_at : tap_at + 1, 0:256], C1))
        slots.append(slot)
    paired = jnp.concatenate(slots, axis=0).T
    small[...] = paired.reshape(4, NXH, NY, NZ, 128)
    core_small = core_start((small, c_small), (delta_grad, c_delta))

    settle(first_ds)
    first_sum(h_ds_lo, h_ds_hi, x_ds_lo, x_ds_hi, n_ds_lo, n_ds_hi)
    second_ds = second_start(n_ds_lo, n_ds_hi, y_ds_lo, y_ds_hi)

    settle(core_small)
    for lo in range(NXL):
        h_small[lo] = small[lo * NC + core] + c_small[lo]
        h_delta[lo] = delta_grad[lo * NC + core] + c_delta[lo]
    first_small = []
    for t in range(1, 4):
        other_hi, other_lo, peer = x_peer(t)
        first_small.append(ship(h_delta.at[other_lo], x_delta.at[x], peer))
        first_small.append(ship(h_small.at[other_lo, other_hi], x_small.at[t - 1], peer))
    x_delta[x] = h_delta[x_lo]

    settle(first_ud)
    first_sum(h_ud_lo, h_ud_hi, x_ud_lo, x_ud_hi, n_ud_lo, n_ud_hi)
    second_ud = second_start(n_ud_lo, n_ud_hi, y_ud_lo, y_ud_hi)

    settle(first_small)
    n_delta[...] = (x_delta[0] + x_delta[1]) + (x_delta[2] + x_delta[3])
    n_small[...] = (h_small[x_lo, x_hi] + x_small[0]) + (x_small[1] + x_small[2])
    second_small = []
    for t in range(1, 4):
        other, peer = y_peer(t)
        second_small.append(ship(n_delta, y_delta.at[y], peer))
        second_small.append(ship(n_small.at[other], y_small.at[t - 1], peer))
    y_delta[y] = n_delta[...]

    settle(second_ds)
    second_sum(n_ds_lo, n_ds_hi, y_ds_lo, y_ds_hi, rows_ds)
    stage[:, 12:16] = jnp.zeros((NZ, 4, WIDE), F32)
    for k in range(NZ):
        stage[k, 0:6] = rows_ds[6 * k : 6 * k + 6]
    settle(second_ud)
    second_sum(n_ud_lo, n_ud_hi, y_ud_lo, y_ud_hi, rows_ud)
    for k in range(NZ):
        stage[k, 6:12] = rows_ud[6 * k : 6 * k + 6]
    settle(second_small)
    rows_small[...] = (n_small[y] + y_small[0]) + (y_small[1] + y_small[2])
    for k in range(NZ):
        stage[k, 12:13, 0:128] = rows_small[k : k + 1]
    low[...] = stage[...].astype(BF16)
    low_delta[z] = ((y_delta[0] + y_delta[1]) + (y_delta[2] + y_delta[3])).astype(BF16)

    sent = []
    for t in range(1, NZ):
        other, peer = z_peer(t)
        sent.append(ship(low_delta.at[z], low_delta.at[z], peer))
        sent.append(ship(low.at[other], got_z.at[t - 1], peer))
    settle(sent)
    total = stage[z]
    for t in range(NZ - 1):
        total = total + got_z[t].astype(F32)
    shares[strip] = total
    total = low_delta[0].astype(F32)
    for k in range(1, NZ):
        total = total + low_delta[k].astype(F32)
    square = total * total
    for channel in range(3):
        misc[channel] = total[8 * channel : 8 * channel + 8]
    misc[4 + strip] = square[0:8] + square[8:16] + square[16:24]

    sent = []
    for t in range(1, 4):
        peer = (dp, strip_peer(t))
        sent.append(ship(shares.at[strip], shares.at[strip], peer))
        sent.append(ship(misc.at[4 + strip], misc.at[4 + strip], peer))
    settle(sent)


N_COPIES = 6 + 3 * 4 + 3 * 6 + 3 * 6 + 14 + 6
N_LOADS = 13


def finish_kernel(
    levels,
    shares,
    misc,
    perturbation,
    loss_out,
    new_out,
    stem_out,
    dw_out,
    up_out,
    down_out,
    ds_out,
    head_out,
):
    loss_out[0] = misc[3][0, 0]
    total = jnp.sum((misc[4] + misc[5]) + (misc[6] + misc[7]))
    spread = jnp.sqrt(jnp.full((8, 128), total, F32) * (1.0 / 12288) + EPS_ROOT)
    for channel in range(3):
        level = STEP_UNIT * levels[channel].astype(F32)
        step = level * misc[channel] / spread
        new_out[channel] = jnp.clip(perturbation[channel] + step, -BOUND, BOUND)
    up_out[0:6] = shares[0, 6:12, 0:C1]
    up_out[6:12] = shares[1, 6:12, 0:C1]
    down_out[0:6] = shares[2, 6:12, 0:C1]
    down_out[6:12] = shares[3, 6:12, 0:C1]
    for place in range(4):
        ds_out[:, place * C1 : (place + 1) * C1] = shares[place, 0:6, 0:C1]
    head_out[...] = shares[0, 0:6, C1 : C1 + CLASSES]
    stem_out[0:1] = shares[0, 12:13, 0:48]
    stem_out[1:2] = shares[0, 12:13, 64 : 64 + 48]
    stem_out[2:3] = shares[1, 12:13, 0:48]
    dw_out[0:1] = shares[1, 12:13, 64 : 64 + 49]
    dw_out[1:2] = shares[2, 12:13, 0:49]
    dw_out[2:3] = shares[2, 12:13, 64 : 64 + 49]


VMEM = pl.BlockSpec(memory_space=pltpu.VMEM)
SMEM = pl.BlockSpec(memory_space=pltpu.SMEM)
ANY = pl.BlockSpec(memory_space=pl.ANY)


def shaped(shape, dtype):
    return jax.ShapeDtypeStruct(shape, dtype)


def run_step(labels, head_gain, *operands):
    strips, parts = NXL * NC, (NXL, NXH, NY, PIECE, 128)

    def low_and_high(first, second):
        return [pltpu.VMEM(first, BF16), pltpu.VMEM(second, BF16)]

    f32 = lambda *shape: pltpu.VMEM(shape, F32)
    bf16 = lambda *shape: pltpu.VMEM(shape, BF16)
    lo, hi = (NXH, NY, PIECE, 128), (NY, NXH, PIECE, 128)
    scratch = [
        bf16(4, 3, 8, 128),
        f32(4, 3, 8, 128),
        pltpu.VMEM((8, F1), jnp.int32),
        bf16(48, C1),
        f32(1, C1),
        bf16(KS * KS, C1),
        f32(1, C1),
        bf16(C1, F1),
        bf16(C1, F1),
        f32(1, C1),
        f32(1, C1),
        bf16(4 * C1, C2),
        bf16(CLASSES, C2),
        f32(ROWS, COLS + 16, C1),
        f32(KS, ROWS, COLS, C1),
        f32(ROWS, COLS, C1),
        bf16(CELLS, WIDE),
        bf16(CELLS, WIDE),
        bf16(CELLS, WIDE),
        f32(64, C1),
        f32(KS * KS, C1),
        bf16(F1, F1),
        bf16(C2, C2),
    ]
    for count in (strips, NXL):
        scratch += [bf16(count, *lo), bf16(count, *hi)] * 2
        scratch += [f32(count, NXH, NY, NZ, 128), f32(count, 24, 128)]
    scratch += [bf16(NXL, *lo), bf16(NY, NXL, NXH, PIECE, 128)] * 2
    scratch += [f32(NXL, NXH, NY, NZ, 128), f32(NXL, 24, 128)]
    scratch += [bf16(3, NY, PIECE, 128), bf16(3, NXL, NXH, PIECE, 128)] * 2
    scratch += [f32(3, NY, NZ, 128), f32(NX, 24, 128)]
    scratch += [bf16(NY, PIECE, 128), bf16(NXL, NXH, PIECE, 128)] * 2
    scratch += [f32(NY, NZ, 128), f32(24, 128)]
    scratch += [bf16(3, PIECE, 128)] * 4 + [f32(3, NZ, 128), f32(NY, 24, 128)]
    scratch += [f32(PIECE, WIDE)] * 2 + [f32(NZ, 128)]
    scratch += [f32(NZ, 16, WIDE), bf16(NZ, 16, WIDE), bf16(NZ - 1, 16, WIDE), bf16(NZ, 24, 128)]
    scratch += [
        pltpu.SemaphoreType.DMA((N_LOADS,)),
        pltpu.SemaphoreType.DMA((N_COPIES,)),
        pltpu.SemaphoreType.DMA((N_COPIES,)),
    ]
    return pl.pallas_call(
        step_kernel,
        name="image_step_and_reduce",
        out_shape=(shaped((4, 16, WIDE), F32), shaped((8, 8, 128), F32)),
        in_specs=[SMEM, VMEM] + [ANY] * len(operands),
        out_specs=(VMEM, VMEM),
        scratch_shapes=scratch,
        compiler_params=pltpu.CompilerParams(
            collective_id=0, has_side_effects=True, vmem_limit_bytes=60 * 1024 * 1024
        ),
    )(labels, head_gain, *operands)


def run_finish(levels, shares, misc, perturbation):
    return pl.pallas_call(
        finish_kernel,
        name="finish",
        out_shape=(
            shaped((1,), F32),
            shaped((3, 8, 128), F32),
            shaped((3, 48), F32),
            shaped((3, KS * KS), F32),
            shaped((12, C1), F32),
            shaped((12, C1), F32),
            shaped((6, 4 * C1), F32),
            shaped((6, CLASSES), F32),
        ),
        in_specs=[SMEM] + [VMEM] * 3,
        out_specs=(SMEM,) + (VMEM,) * 7,
    )(levels, shares, misc, perturbation)


def on_device(
    images,
    perturbation,
    labels,
    step_levels,
    stem_weight,
    stem_gain,
    dw1_kernel,
    norm1_gain,
    up1_weight,
    down1_weight,
    scale1,
    down_gain,
    ds_weight,
    head_gain,
    head_weight,
):
    shares, misc = run_step(
        labels,
        head_gain,
        images,
        perturbation,
        jnp.asarray(index_table()),
        stem_weight,
        stem_gain.reshape(1, C1),
        dw1_kernel,
        norm1_gain.reshape(1, C1),
        up1_weight,
        down1_weight.T,
        scale1.reshape(1, C1),
        down_gain.reshape(1, C1),
        ds_weight,
        head_weight.T,
    )
    loss, new_delta, stem, dw, up, down, ds, head = run_finish(
        step_levels, shares, misc, perturbation
    )
    return (new_delta, loss, stem.T, dw.T, up.T, down, ds.T, head)


def solution(mesh):
    return jax.shard_map(
        on_device,
        mesh=mesh,
        in_specs=(
            P("dp", None, "strip", None),
            P(None, "strip", None),
            P(("dp", "strip")),
        )
        + (P(),) * 12,
        out_specs=(
            P(None, "strip", None),
            P(("dp", "strip")),
            P(None, "dp"),
            P(None, "dp"),
            P(None, "dp"),
            P("dp", None),
            P(None, "dp"),
            P("dp", None),
        ),
        check_vma=False,
    )
```

```python
import jax
import jax.numpy as jnp
import numpy as np
from jax import lax
from jax.experimental import pallas as pl
from jax.experimental.pallas import tpu as pltpu
from jax.sharding import PartitionSpec as P

KS = 7
EPS_NORM = 1e-06
EPS_ROOT = 1e-12
BOUND = 0.5
STEP_UNIT = 0.1

NZ, NY, NXH, NXL, NC = 8, 4, 2, 2, 2
NX = NXH * NXL
ROWS, COLS, CELLS = 8, 32, 256
C1, F1, C2, CLASSES = 192, 768, 384, 62
WIDE = 256
PIECE = 48

F32 = jnp.float32
BF16 = jnp.bfloat16
MESH = pl.DeviceIdType.MESH


def index_table():
    table = np.full((16, F1), -1, np.int32)
    slots = {(0, 0): (2, 0), (0, 1): (6, 1), (1, 0): (2, 2), (1, 1): (7, 0), (2, 0): (3, 1), (2, 1): (7, 2)}
    for x_hi in range(NXH):
        for y in range(NY):
            for z in range(NZ):
                own = (z * NY + y) * NXH + x_hi
                block = (x_hi * NY + y) * NZ + z
                for q in range(6):
                    table[0, 6 * block + q] = own * 12 + q
                    table[0, 384 + 6 * block + q] = own * 12 + 6 + q
                    table[1, 6 * block + q] = own * 6 + q
                    table[8, 6 * block + q] = x_hi * NY + y
                    table[9, 6 * block + q] = 64 + z * 6 + q
                for (strip, _), (row, column) in slots.items():
                    table[row, strip * 64 + block] = own * 3 + column
    for part_col in range(4):
        for strip in range(4):
            for channel in range(3):
                for row in range(8):
                    lane = part_col * 128 + strip * 24 + channel * 8 + row
                    table[4, lane] = channel * 16 + (row % 4) * 4 + part_col
                    table[5, lane] = strip * 2 + row // 4
    return table


def dot_nn(a, b):
    return lax.dot_general(a, b, (((1,), (0,)), ((), ())), preferred_element_type=F32)


def dot_nt(a, b):
    return lax.dot_general(a, b, (((1,), (1,)), ((), ())), preferred_element_type=F32)


def dot_tn(a, b):
    return lax.dot_general(a, b, (((0,), (0,)), ((), ())), preferred_element_type=F32)


def mean_lanes(values):
    return jnp.sum(values, axis=-1, keepdims=True) * (1.0 / values.shape[-1])


def norm_parts(values):
    centred = values - mean_lanes(values)
    root = lax.rsqrt(mean_lanes(centred * centred) + EPS_NORM)
    return centred * root, root


def norm_back(unit, root, grad):
    return root * (grad - mean_lanes(grad) - unit * mean_lanes(grad * unit))


def one_hot(index_row, rows):
    width = index_row.shape[1]
    return (lax.broadcasted_iota(jnp.int32, (rows, width), 0) == index_row).astype(F32).astype(BF16)


def step_kernel(
    label_in,
    head_gain_in,
    images,
    strip_delta,
    table_in,
    stem_in,
    stem_gain_in,
    taps_in,
    norm1_in,
    up_in,
    down_in,
    scale_in,
    down_gain_in,
    ds_in,
    head_in_t,
    shares,
    misc,
    label,
    head_gain,
    own_images,
    own_delta,
    own_pixels,
    pixels,
    table,
    stem_weight,
    stem_gain,
    taps,
    norm1_gain,
    up_weight,
    down_weight,
    scale1,
    down_gain,
    ds_weight,
    head_weight,
    padded,
    shifted,
    mixed_ref,
    wide_merged,
    wide_normed,
    wide_branch,
    tap_grad,
    taps_ref,
    up_ordered,
    down_ordered,
    unit_pick,
    column_pick,
    feature_pick,
    fold,
    slot_pick,
    factors,
    ud,
    small,
    delta_grad,
    c_ud,
    c_small,
    c_delta,
    h_ud,
    h_late,
    got_factors,
    x_ud,
    x_late,
    rows_ds,
    rows_ud,
    rows_late,
    stage,
    low,
    got_z,
    low_delta,
    local,
    send,
    recv,
):
    dp, strip = lax.axis_index("dp"), lax.axis_index("strip")
    z, y, x_hi = dp // (NY * NXH), (dp // NXH) % NY, dp % NXH
    x_lo, core = strip // NC, strip % NC
    x = x_hi * NXL + x_lo

    plane_steps = sorted(
        ((i, j) for i in range(NX) for j in range(NY) if i or j),
        key=lambda step: -(min(step[0], NX - step[0]) + min(step[1], NY - step[1])),
    )

    def plane_peer(step):
        other, other_y = (x + step[0]) % NX, (y + step[1]) % NY
        other_hi, other_lo = other // NXL, other % NXL
        other_dp = (z * NY + other_y) * NXH + other_hi
        same, crossed = (other_dp, other_lo * NC + core), (other_dp, other_lo * NC + 1 - core)
        return other_lo, other_hi, other_y, same, crossed

    def z_peer(t):
        other = (z + t) % NZ
        return other, ((other * NY + y) * NXH + x_hi, strip)

    def strip_peer(t):
        return (strip + t) % (NXL * NC)

    barrier = pltpu.get_barrier_semaphore()
    peers = [(dp, strip_peer(t)) for t in range(1, 4)]
    peers += [plane_peer(step)[3] for step in plane_steps]
    peers += [plane_peer(step)[4] for step in plane_steps]
    peers += [z_peer(t)[1] for t in range(1, NZ)]
    for peer in peers:
        pl.semaphore_signal(barrier, inc=1, device_id=peer, device_id_type=MESH)

    loads = {}
    for k, (name, source, target) in enumerate(
        (
            ("images", images, own_images),
            ("delta", strip_delta, own_delta),
            ("table", table_in, table),
            ("label", label_in, label),
            ("head_gain", head_gain_in, head_gain),
            ("stem", stem_in, stem_weight),
            ("stem_gain", stem_gain_in, stem_gain),
            ("taps", taps_in, taps),
            ("norm1", norm1_in, norm1_gain),
            ("up", up_in, up_weight),
            ("down", down_in, down_weight),
            ("scale", scale_in, scale1),
            ("down_gain", down_gain_in, down_gain),
            ("ds", ds_in, ds_weight),
            ("head", head_in_t, head_weight),
        )
    ):
        loads[name] = pltpu.make_async_copy(source, target, local.at[k])
        loads[name].start()

    count = [0]

    def ship(source, target, peer):
        k = count[0]
        count[0] += 1
        copy = pltpu.make_async_remote_copy(
            src_ref=source,
            dst_ref=target,
            send_sem=send.at[k],
            recv_sem=recv.at[k],
            device_id=peer,
            device_id_type=MESH,
        )
        copy.start()
        return copy

    def settle(copies):
        for copy in copies:
            copy.wait()

    wide_merged[...] = jnp.zeros((CELLS, WIDE), BF16)
    wide_normed[...] = jnp.zeros((CELLS, WIDE), BF16)
    wide_branch[...] = jnp.zeros((CELLS, WIDE), BF16)
    tap_grad[...] = jnp.zeros_like(tap_grad)
    padded[:, 0:8, :] = jnp.zeros((ROWS, 8, C1), F32)
    padded[:, 8 + COLS :, :] = jnp.zeros((ROWS, 8, C1), F32)
    loads["table"].wait()
    hidden_pick = one_hot(table[0:1, :], F1)
    loads["up"].wait()
    up_ordered[...] = dot_nn(up_weight[...], hidden_pick).astype(BF16)
    loads["down"].wait()
    down_ordered[...] = dot_nn(down_weight[...], hidden_pick).astype(BF16)
    unit_pick[...] = one_hot(table[1:2, 0:C2], C2)
    feature_pick[...] = one_hot(table[4:5, 0:512], 48)
    fold[...] = one_hot(table[9:10, 0:C2], 128)
    for k, row in enumerate((2, 3, 6, 7)):
        slot_pick[k] = one_hot(table[row : row + 1, 0:256], C1)
    i0 = lax.broadcasted_iota(jnp.int32, (128, 128), 0)
    i1 = lax.broadcasted_iota(jnp.int32, (128, 128), 1)
    column_pick[...] = (i1 == 4 * (i0 & 31) + (i0 >> 5)).astype(F32).astype(BF16)
    loads["taps"].wait()
    taps_ref[...] = taps[...].astype(F32)
    loads["images"].wait()
    loads["delta"].wait()
    own_pixels[...] = (own_images[...].astype(F32) + own_delta[...]).astype(BF16)
    pl.semaphore_wait(barrier, len(peers))

    sent = []
    for t in range(1, 4):
        peer = strip_peer(t)
        sent.append(ship(own_pixels.at[peer], pixels.at[strip], (dp, peer)))
    pixels[strip] = own_pixels[strip]
    for name in (
        "label", "head_gain", "stem", "stem_gain", "norm1", "scale", "down_gain", "ds", "head"
    ):
        loads[name].wait()
    settle(sent)

    perturbed = pixels[...].astype(F32).reshape(96, 128)
    perturbed = jnp.concatenate([perturbed, jnp.zeros((32, 128), F32)], axis=0).astype(BF16)
    columns = dot_nt(column_pick[...], perturbed)
    columns = jnp.concatenate([columns[32 * k : 32 * k + 32] for k in range(4)], axis=1)
    row_of = table[5:6, 0:512]
    cells = jnp.concatenate(
        [jnp.where(row_of == r, columns, 0.0) for r in range(ROWS)], axis=0
    ).astype(BF16)
    patches = dot_nt(cells, feature_pick[...]).astype(BF16)

    stem_pre = dot_nn(patches, stem_weight[...])
    stem_unit, stem_root = norm_parts(stem_pre)
    stem_out = (stem_unit * stem_gain[...]).astype(BF16).astype(F32)

    def spread_columns(values):
        padded[:, 8 : 8 + COLS, :] = values.reshape(ROWS, COLS, C1)
        for j in range(KS):
            shifted[j] = padded[:, 5 + j : 5 + j + COLS, :]

    def correlate(tap_of):
        for r in range(ROWS):
            total = None
            for i in range(KS):
                if 0 <= r + i - 3 < ROWS:
                    for j in range(KS):
                        tap = tap_of(i, j)
                        term = shifted[j, r + i - 3] * taps_ref[tap : tap + 1, :]
                        total = term if total is None else total + term
            mixed_ref[r] = total
        return mixed_ref[...].reshape(CELLS, C1)

    spread_columns(stem_out)
    mixed = correlate(lambda i, j: KS * i + j)

    mixed_unit, mixed_root = norm_parts(mixed)
    normed = (mixed_unit * norm1_gain[...]).astype(BF16)
    wide_normed[:, 0:C1] = normed
    upper = dot_nn(normed, up_ordered[...])
    half = 0.5 + 0.5 * lax.erf(upper * (0.5**0.5))
    hidden = (upper * half).astype(BF16)
    gelu_slope = half + upper * jnp.exp(-0.5 * upper * upper) * ((2.0 * np.pi) ** -0.5)
    branch = dot_nt(hidden, down_ordered[...])
    section = (stem_out + scale1[...] * branch).astype(BF16).astype(F32)

    section_unit, section_root = norm_parts(section)
    wide_merged[:, 0:C1] = (section_unit * down_gain[...]).astype(BF16)
    p0 = lax.broadcasted_iota(jnp.int32, (16, CELLS), 0)
    p1 = lax.broadcasted_iota(jnp.int32, (16, CELLS), 1)
    place_pick = (p0 == 2 * ((p1 >> 5) & 1) + (p1 & 1)).astype(F32).astype(BF16)
    merged_sum = dot_nn(place_pick, wide_merged[...])
    sums_high = merged_sum.astype(BF16).astype(F32)
    rest = merged_sum - sums_high
    sums_mid = rest.astype(BF16).astype(F32)
    sums_low = rest - sums_mid
    row16 = lax.broadcasted_iota(jnp.int32, (16, WIDE), 0)

    def place_rows(place):
        high = sums_high[place : place + 1]
        mid = sums_mid[place : place + 1]
        lowest = sums_low[place : place + 1]
        return jnp.where(
            row16 == 0, high, jnp.where(row16 == 1, mid, jnp.where(row16 == 2, lowest, 0.0))
        ).astype(BF16)

    split_sums = [place_rows(place) for place in range(4)]
    pooled = None
    for place in range(4):
        term = dot_nn(split_sums[place][:, 0:C1], ds_weight[place * C1 : (place + 1) * C1, :])
        pooled = term if pooled is None else pooled + term
    cells_two = CELLS // 4
    pooled = jnp.sum(pooled, axis=0, keepdims=True) * (1.0 / cells_two)
    pooled = jnp.broadcast_to(pooled, (16, C2))
    head_unit, head_root = norm_parts(pooled)
    gain = head_gain[...].reshape(1, C2)
    head_in = (head_unit * gain).astype(BF16)
    logits = dot_nt(head_in, head_weight[...])
    onehot = (lax.broadcasted_iota(jnp.int32, logits.shape, 1) == label[0]).astype(F32)
    top = jnp.max(logits, axis=-1, keepdims=True)
    raised = jnp.exp(logits - top)
    mass = jnp.sum(raised, axis=-1, keepdims=True)
    losses = jnp.log(mass) + top - jnp.sum(onehot * logits, axis=-1, keepdims=True)
    misc[3] = jnp.broadcast_to(losses[0:8], (8, 128))
    grad_logits = (raised / mass - onehot).astype(BF16)
    grad_head_in = dot_nn(grad_logits, head_weight[...])
    grad_pooled = norm_back(head_unit, head_root, grad_head_in * gain)
    grad_start = (grad_pooled * (1.0 / cells_two)).astype(BF16)

    block_of = lax.broadcasted_iota(jnp.int32, (16, C2), 0) == table[8:9, 0:C2]
    start_rows = jnp.where(block_of, dot_nn(grad_start, unit_pick[...]), 0.0).astype(BF16)
    start_blocks = dot_nt(start_rows, fold[...])
    head_rows = jnp.where(block_of, dot_nn(head_in, unit_pick[...]), 0.0).astype(BF16)
    head_blocks = dot_nt(head_rows, fold[...])
    e0 = lax.broadcasted_iota(jnp.int32, (CLASSES, 128), 0)
    e1 = lax.broadcasted_iota(jnp.int32, (CLASSES, 128), 1)
    logit_row = dot_nn(grad_logits, (e0 == e1).astype(F32).astype(BF16))[0:1]
    row8 = lax.broadcasted_iota(jnp.int32, (8, 128), 0)
    for hi in range(NXH):
        for k in range(NY):
            at = hi * NY + k
            third = jnp.where(row8 == 2, logit_row + head_blocks[at : at + 1], 0.0)
            for place in range(4):
                second = merged_sum[place : place + 1, 128:256] + start_blocks[at : at + 1]
                first = merged_sum[place : place + 1, 0:128]
                factors[place, hi, k] = jnp.where(row8 == 0, first, jnp.where(row8 == 1, second, third))
    mine = (x * NY + y) * NC + core
    factor_copies = []
    for step in plane_steps:
        other_lo, other_hi, other_y, same, crossed = plane_peer(step)
        for other_core, peer in ((core, same), (1 - core, crossed)):
            source = factors.at[other_lo * NC + other_core, other_hi, other_y]
            factor_copies.append(ship(source, got_factors.at[mine], peer))
    partner = (dp, x_lo * NC + (1 - core))
    source = factors.at[x_lo * NC + (1 - core), x_hi, y]
    factor_copies.append(ship(source, got_factors.at[mine], partner))
    got_factors[mine] = factors[strip, x_hi, y]

    def store_rows(blocks, at_strip, grads):
        for hi in range(NXH):
            for k in range(NY):
                at = (hi * NY + k) * PIECE
                blocks[at_strip, hi, k] = grads[at : at + PIECE].astype(BF16)

    def core_start(*pairs):
        copies = []
        for lo in range(NXL):
            for source, target in pairs:
                copies.append(ship(source.at[lo * NC + (1 - core)], target.at[lo], partner))
        return copies

    def core_sum(own, got, held):
        for lo in range(NXL):
            block = own[lo * NC + core].astype(F32) + got[lo].astype(F32)
            held[lo] = block.astype(BF16)

    def plane_start(held, got):
        copies = []
        for k, step in enumerate(plane_steps):
            other_lo, other_hi, other_y, peer, _ = plane_peer(step)
            copies.append(ship(held.at[other_lo, other_hi, other_y], got.at[k], peer))
        return copies

    def plane_sum(held, got, rows):
        total = held[x_lo, x_hi, y].astype(F32)
        for k in range(len(plane_steps)):
            total = total + got[k].astype(F32)
        rows[...] = total

    place_grads = [
        dot_nt(grad_start, ds_weight[place * C1 : (place + 1) * C1, :])[0:1] * down_gain[...]
        for place in range(4)
    ]
    even = (lax.broadcasted_iota(jnp.int32, (COLS, C1), 0) & 1) == 0
    by_row = [
        jnp.where(even, place_grads[2 * k], place_grads[2 * k + 1]) for k in range(2)
    ]
    grad_unit = jnp.concatenate([by_row[r % 2] for r in range(ROWS)], axis=0)
    grad_block = norm_back(section_unit, section_root, grad_unit).astype(BF16).astype(F32)

    grad_branch = (grad_block * scale1[...]).astype(BF16)
    wide_branch[:, 0:C1] = grad_branch
    grad_down = dot_tn(hidden, wide_branch[...])
    store_rows(ud, 2, grad_down[0:384])
    store_rows(ud, 3, grad_down[384:768])
    grad_hidden = dot_nn(grad_branch, down_ordered[...])
    grad_upper = (grad_hidden * gelu_slope).astype(BF16)
    grad_up = dot_tn(grad_upper, wide_normed[...])
    store_rows(ud, 0, grad_up[0:384])
    store_rows(ud, 1, grad_up[384:768])
    core_ud = core_start((ud, c_ud))

    grad_normed = dot_nt(grad_upper, up_ordered[...])
    grad_mixed = norm_back(mixed_unit, mixed_root, grad_normed * norm1_gain[...])

    mixed_ref[...] = grad_mixed.reshape(ROWS, COLS, C1)
    for i in range(KS):
        for j in range(KS):
            total = None
            for r in range(ROWS):
                if 0 <= r + i - 3 < ROWS:
                    term = shifted[j, r + i - 3] * mixed_ref[r]
                    total = term if total is None else total + term
            tap = KS * i + j
            tap_grad[tap : tap + 1, :] = jnp.sum(total, axis=0, keepdims=True)

    settle(core_ud)
    core_sum(ud, c_ud, h_ud)
    plane_ud = plane_start(h_ud, x_ud)

    spread_columns(grad_mixed)
    grad_stem = grad_block + correlate(lambda i, j: KS * (KS - 1 - i) + (KS - 1 - j))
    grad_pre = norm_back(stem_unit, stem_root, grad_stem * stem_gain[...]).astype(BF16)

    grad_patches = dot_nt(grad_pre, stem_weight[...]).astype(BF16)
    grad_cells = dot_nn(grad_patches, feature_pick[...])
    grad_columns = None
    for r in range(ROWS):
        term = jnp.where(row_of == r, grad_cells[r * COLS : (r + 1) * COLS], 0.0)
        grad_columns = term if grad_columns is None else grad_columns + term
    grad_columns = grad_columns.astype(BF16)
    grad_pixels = None
    for k in range(4):
        term = dot_tn(
            grad_columns[:, 128 * k : 128 * k + 128], column_pick[32 * k : 32 * k + 32, :]
        )
        grad_pixels = term if grad_pixels is None else grad_pixels + term
    delta_grad[...] = grad_pixels[0:96].reshape(4, 24, 128).astype(BF16)

    stem_low = dot_tn(patches, grad_pre)
    stem_low = jnp.concatenate([stem_low, jnp.zeros((16, C1), F32)], axis=0).astype(BF16)
    tap_low = tap_grad[...].astype(BF16)
    slots = []
    for k in range(2):
        slots.append(dot_nn(stem_low, slot_pick[2 * k]) + dot_nn(tap_low, slot_pick[2 * k + 1]))
    paired = jnp.concatenate(slots, axis=0).T
    small[...] = paired.reshape(4, NXH, NY, NZ, 128)
    core_small = core_start((small, c_small), (delta_grad, c_delta))

    settle(core_small)
    for lo in range(NXL):
        mine = lo * NC + core
        block = delta_grad[mine].astype(F32) + c_delta[lo].astype(F32)
        late = small[mine] + c_small[lo]
        for hi in range(NXH):
            for k in range(NY):
                h_late[lo, hi, k] = jnp.concatenate([block, late[hi, k]], axis=0).astype(BF16)
    plane_late = []
    mine = x * NY + y
    for step in plane_steps:
        other_lo, other_hi, other_y, peer, _ = plane_peer(step)
        plane_late.append(ship(h_late.at[other_lo, other_hi, other_y], x_late.at[mine], peer))
    x_late[mine] = h_late[x_lo, x_hi, y]

    settle(factor_copies)
    low_half, high_half = got_factors[:, 0, :], got_factors[:, 1, :]
    third = got_factors[:, 2, :]
    first_lanes = lax.broadcasted_iota(jnp.int32, high_half.shape, 1) < 64
    sums = jnp.concatenate([low_half, jnp.where(first_lanes, high_half, 0.0)], axis=1)
    sums_high = sums.astype(BF16)
    sums_low = (sums - sums_high.astype(F32)).astype(BF16)
    starts = high_half.astype(BF16)
    o0 = lax.broadcasted_iota(jnp.int32, (128, WIDE), 0)
    o1 = lax.broadcasted_iota(jnp.int32, (128, WIDE), 1)
    head_offset = ((o1 == o0 + C1) & (o0 < 64)).astype(F32).astype(BF16)
    third = third.astype(BF16)
    placed_logits = dot_nn(third, head_offset).astype(BF16)
    products = dot_tn(starts, sums_high) + dot_tn(starts, sums_low) + dot_tn(third, placed_logits)
    rows_ds[...] = products[64 : 64 + PIECE]
    stage[:, 12:16] = jnp.zeros((NZ, 4, WIDE), F32)
    for k in range(NZ):
        stage[k, 0:6] = rows_ds[6 * k : 6 * k + 6]
    settle(plane_ud)
    plane_sum(h_ud, x_ud, rows_ud)
    for k in range(NZ):
        stage[k, 6:12] = rows_ud[6 * k : 6 * k + 6]
    settle(plane_late)
    total = x_late[0].astype(F32)
    for k in range(1, NX * NY):
        total = total + x_late[k].astype(F32)
    rows_late[...] = total[24:32]
    low_delta[z] = total[0:24].astype(BF16)
    for k in range(NZ):
        stage[k, 12:13, 0:128] = rows_late[k : k + 1]
    low[...] = stage[...].astype(BF16)

    sent = []
    for t in range(1, NZ):
        other, peer = z_peer(t)
        sent.append(ship(low_delta.at[z], low_delta.at[z], peer))
        sent.append(ship(low.at[other], got_z.at[t - 1], peer))
    settle(sent)
    total = stage[z]
    for t in range(NZ - 1):
        total = total + got_z[t].astype(F32)
    shares[strip] = total.astype(BF16)
    total = low_delta[0].astype(F32)
    for k in range(1, NZ):
        total = total + low_delta[k].astype(F32)
    square = total * total
    for channel in range(3):
        misc[channel] = total[8 * channel : 8 * channel + 8]
    misc[4 + strip] = square[0:8] + square[8:16] + square[16:24]

    sent = []
    for t in range(1, 4):
        peer = (dp, strip_peer(t))
        sent.append(ship(shares.at[strip], shares.at[strip], peer))
        sent.append(ship(misc.at[4 + strip], misc.at[4 + strip], peer))
    settle(sent)


N_COPIES = 3 + 31 + 2 + 4 + 2 * 15 + 14 + 6
N_LOADS = 15


def finish_kernel(
    levels,
    shares,
    misc,
    perturbation,
    loss_out,
    new_out,
    stem_out,
    dw_out,
    up_out,
    down_out,
    ds_out,
    head_out,
):
    loss_out[0] = misc[3][0, 0]
    share = [shares[place].astype(F32) for place in range(4)]
    total = jnp.sum((misc[4] + misc[5]) + (misc[6] + misc[7]))
    spread = jnp.sqrt(jnp.full((8, 128), total, F32) * (1.0 / 12288) + EPS_ROOT)
    for channel in range(3):
        level = STEP_UNIT * levels[channel].astype(F32)
        step = level * misc[channel] / spread
        new_out[channel] = jnp.clip(perturbation[channel] + step, -BOUND, BOUND)
    up_out[0:6] = share[0][6:12, 0:C1]
    up_out[6:12] = share[1][6:12, 0:C1]
    down_out[0:6] = share[2][6:12, 0:C1]
    down_out[6:12] = share[3][6:12, 0:C1]
    for place in range(4):
        ds_out[:, place * C1 : (place + 1) * C1] = share[place][0:6, 0:C1]
    head_out[...] = share[0][0:6, C1 : C1 + CLASSES]
    stem_out[0:1] = share[0][12:13, 0:48]
    stem_out[1:2] = share[0][12:13, 64 : 64 + 48]
    stem_out[2:3] = share[1][12:13, 0:48]
    dw_out[0:1] = share[1][12:13, 64 : 64 + 49]
    dw_out[1:2] = share[2][12:13, 0:49]
    dw_out[2:3] = share[2][12:13, 64 : 64 + 49]


VMEM = pl.BlockSpec(memory_space=pltpu.VMEM)
SMEM = pl.BlockSpec(memory_space=pltpu.SMEM)
ANY = pl.BlockSpec(memory_space=pl.ANY)


def shaped(shape, dtype):
    return jax.ShapeDtypeStruct(shape, dtype)


def run_step(*operands):
    strips = NXL * NC
    f32 = lambda *shape: pltpu.VMEM(shape, F32)
    bf16 = lambda *shape: pltpu.VMEM(shape, BF16)
    scratch = [
        pltpu.SMEM((1,), jnp.int32),
        f32(C2),
        bf16(4, 3, 8, 128),
        f32(3, 8, 128),
        bf16(4, 3, 8, 128),
        bf16(4, 3, 8, 128),
        pltpu.VMEM((16, F1), jnp.int32),
        bf16(48, C1),
        f32(1, C1),
        bf16(KS * KS, C1),
        f32(1, C1),
        bf16(C1, F1),
        bf16(C1, F1),
        f32(1, C1),
        f32(1, C1),
        bf16(4 * C1, C2),
        bf16(CLASSES, C2),
        f32(ROWS, COLS + 16, C1),
        f32(KS, ROWS, COLS, C1),
        f32(ROWS, COLS, C1),
        bf16(CELLS, WIDE),
        bf16(CELLS, WIDE),
        bf16(CELLS, WIDE),
        f32(64, C1),
        f32(KS * KS, C1),
        bf16(C1, F1),
        bf16(C1, F1),
        bf16(C2, C2),
        bf16(128, 128),
        bf16(48, 512),
        bf16(128, C2),
        bf16(4, C1, 256),
    ]
    plane = NX * NY
    scratch += [f32(strips, NXH, NY, 8, 128)]
    for count in (strips, NXL):
        scratch += [bf16(count, NXH, NY, PIECE, WIDE)]
        scratch += [f32(count, NXH, NY, NZ, 128), bf16(count, 24, 128)]
    scratch += [bf16(NXL, NXH, NY, PIECE, WIDE), bf16(NXL, NXH, NY, 32, 128)]
    scratch += [f32(plane * NC, 8, 128), bf16(plane - 1, PIECE, WIDE), bf16(plane, 32, 128)]
    scratch += [f32(PIECE, WIDE)] * 2 + [f32(NZ, 128)]
    scratch += [f32(NZ, 16, WIDE), bf16(NZ, 16, WIDE), bf16(NZ - 1, 16, WIDE), bf16(NZ, 24, 128)]
    scratch += [
        pltpu.SemaphoreType.DMA((N_LOADS,)),
        pltpu.SemaphoreType.DMA((N_COPIES,)),
        pltpu.SemaphoreType.DMA((N_COPIES,)),
    ]
    return pl.pallas_call(
        step_kernel,
        name="image_step_and_reduce",
        out_shape=(shaped((4, 16, WIDE), BF16), shaped((8, 8, 128), F32)),
        in_specs=[ANY] * len(operands),
        out_specs=(VMEM, VMEM),
        scratch_shapes=scratch,
        compiler_params=pltpu.CompilerParams(
            collective_id=0, has_side_effects=True, vmem_limit_bytes=60 * 1024 * 1024
        ),
    )(*operands)


def run_finish(levels, shares, misc, perturbation):
    return pl.pallas_call(
        finish_kernel,
        name="finish",
        out_shape=(
            shaped((1,), F32),
            shaped((3, 8, 128), F32),
            shaped((3, 48), F32),
            shaped((3, KS * KS), F32),
            shaped((12, C1), F32),
            shaped((12, C1), F32),
            shaped((6, 4 * C1), F32),
            shaped((6, CLASSES), F32),
        ),
        in_specs=[SMEM] + [VMEM] * 3,
        out_specs=(SMEM,) + (VMEM,) * 7,
    )(levels, shares, misc, perturbation)


def on_device(
    images,
    perturbation,
    labels,
    step_levels,
    stem_weight,
    stem_gain,
    dw1_kernel,
    norm1_gain,
    up1_weight,
    down1_weight,
    scale1,
    down_gain,
    ds_weight,
    head_gain,
    head_weight,
):
    shares, misc = run_step(
        labels,
        head_gain,
        images,
        perturbation,
        jnp.asarray(index_table()),
        stem_weight,
        stem_gain.reshape(1, C1),
        dw1_kernel,
        norm1_gain.reshape(1, C1),
        up1_weight,
        down1_weight.T,
        scale1.reshape(1, C1),
        down_gain.reshape(1, C1),
        ds_weight,
        head_weight.T,
    )
    loss, new_delta, stem, dw, up, down, ds, head = run_finish(
        step_levels, shares, misc, perturbation
    )
    return (new_delta, loss, stem.T, dw.T, up.T, down, ds.T, head)


def solution(mesh):
    return jax.shard_map(
        on_device,
        mesh=mesh,
        in_specs=(
            P("dp", None, "strip", None),
            P(None, "strip", None),
            P(("dp", "strip")),
        )
        + (P(),) * 12,
        out_specs=(
            P(None, "strip", None),
            P(("dp", "strip")),
            P(None, "dp"),
            P(None, "dp"),
            P(None, "dp"),
            P("dp", None),
            P(None, "dp"),
            P("dp", None),
        ),
        check_vma=False,
    )
```

```python
import jax
import jax.numpy as jnp
import numpy as np
from jax import lax
from jax.experimental import pallas as pl
from jax.experimental.pallas import tpu as pltpu
from jax.sharding import PartitionSpec as P

KS = 7
EPS_NORM = 1e-06
EPS_ROOT = 1e-12
BOUND = 0.5
STEP_UNIT = 0.1

NZ, NY, NXH, NXL, NC = 8, 4, 2, 2, 2
NX = NXH * NXL
ROWS, COLS, CELLS = 8, 32, 256
C1, F1, C2, CLASSES = 192, 768, 384, 62
WIDE = 256
PIECE = 48
FOLDED = 72

F32 = jnp.float32
BF16 = jnp.bfloat16
MESH = pl.DeviceIdType.MESH


def index_table():
    table = np.full((16, F1), -1, np.int32)
    slots = {(0, 0): (2, 0), (0, 1): (6, 1), (1, 0): (2, 2), (1, 1): (7, 0), (2, 0): (3, 1), (2, 1): (7, 2)}
    for x_hi in range(NXH):
        for y in range(NY):
            for z in range(NZ):
                own = (z * NY + y) * NXH + x_hi
                block = (x_hi * NY + y) * NZ + z
                for q in range(6):
                    table[0, 6 * block + q] = own * 12 + q
                    table[0, 384 + 6 * block + q] = own * 12 + 6 + q
                    table[1, 6 * block + q] = own * 6 + q
                    table[8, 6 * block + q] = x_hi * NY + y
                    table[9, 6 * block + q] = 64 + z * 6 + q
                for (strip, _), (row, column) in slots.items():
                    table[row, strip * 64 + block] = own * 3 + column
    for part_col in range(4):
        for strip in range(4):
            for channel in range(3):
                for row in range(8):
                    lane = part_col * 128 + strip * 24 + channel * 8 + row
                    table[4, lane] = channel * 16 + (row % 4) * 4 + part_col
                    table[5, lane] = strip * 2 + row // 4
    return table


def dot_nn(a, b):
    return lax.dot_general(a, b, (((1,), (0,)), ((), ())), preferred_element_type=F32)


def dot_nt(a, b):
    return lax.dot_general(a, b, (((1,), (1,)), ((), ())), preferred_element_type=F32)


def dot_tn(a, b):
    return lax.dot_general(a, b, (((0,), (0,)), ((), ())), preferred_element_type=F32)


def mean_lanes(values):
    return jnp.sum(values, axis=-1, keepdims=True) * (1.0 / values.shape[-1])


def norm_parts(values):
    centred = values - mean_lanes(values)
    root = lax.rsqrt(mean_lanes(centred * centred) + EPS_NORM)
    return centred * root, root


def norm_back(unit, root, grad):
    return root * (grad - mean_lanes(grad) - unit * mean_lanes(grad * unit))


def one_hot(index_row, rows):
    width = index_row.shape[1]
    return (lax.broadcasted_iota(jnp.int32, (rows, width), 0) == index_row).astype(F32).astype(BF16)


def step_kernel(
    label_in,
    head_gain_in,
    images,
    strip_delta,
    table_in,
    stem_in,
    stem_gain_in,
    taps_in,
    norm1_in,
    up_in,
    down_in,
    scale_in,
    down_gain_in,
    ds_in,
    head_in_t,
    shares,
    misc,
    label,
    head_gain,
    own_images,
    own_delta,
    own_pixels,
    pixels,
    table,
    stem_weight,
    stem_gain,
    taps,
    norm1_gain,
    up_weight,
    down_weight,
    scale1,
    down_gain,
    ds_weight,
    head_weight,
    padded,
    shifted,
    mixed_ref,
    wide_merged,
    wide_normed,
    wide_branch,
    tap_grad,
    taps_ref,
    up_ordered,
    down_ordered,
    unit_pick,
    column_pick,
    feature_pick,
    fold,
    slot_pick,
    factors,
    ud,
    small,
    delta_grad,
    c_ud,
    c_small,
    c_delta,
    h_ud,
    h_late,
    got_factors,
    x_ud,
    x_late,
    rows_ds,
    rows_ud,
    rows_late,
    stage,
    low,
    got_z,
    low_delta,
    local,
    send,
    recv,
):
    dp, strip = lax.axis_index("dp"), lax.axis_index("strip")
    z, y, x_hi = dp // (NY * NXH), (dp // NXH) % NY, dp % NXH
    x_lo, core = strip // NC, strip % NC
    x = x_hi * NXL + x_lo

    plane_steps = sorted(
        ((i, j) for i in range(NX) for j in range(NY) if i or j),
        key=lambda step: -(min(step[0], NX - step[0]) + min(step[1], NY - step[1])),
    )

    def plane_peer(step):
        other, other_y = (x + step[0]) % NX, (y + step[1]) % NY
        other_hi, other_lo = other // NXL, other % NXL
        other_dp = (z * NY + other_y) * NXH + other_hi
        same, crossed = (other_dp, other_lo * NC + core), (other_dp, other_lo * NC + 1 - core)
        return other_lo, other_hi, other_y, same, crossed

    def z_peer(t):
        other = (z + t) % NZ
        return other, ((other * NY + y) * NXH + x_hi, strip)

    def strip_peer(t):
        return (strip + t) % (NXL * NC)

    barrier = pltpu.get_barrier_semaphore()
    peers = [(dp, strip_peer(t)) for t in range(1, 4)]
    peers += [plane_peer(step)[3] for step in plane_steps]
    peers += [plane_peer(step)[4] for step in plane_steps]
    peers += [z_peer(t)[1] for t in range(1, NZ)]
    for peer in peers:
        pl.semaphore_signal(barrier, inc=1, device_id=peer, device_id_type=MESH)

    loads = {}
    for k, (name, source, target) in enumerate(
        (
            ("images", images, own_images),
            ("delta", strip_delta, own_delta),
            ("table", table_in, table),
            ("label", label_in, label),
            ("head_gain", head_gain_in, head_gain),
            ("stem", stem_in, stem_weight),
            ("stem_gain", stem_gain_in, stem_gain),
            ("taps", taps_in, taps),
            ("norm1", norm1_in, norm1_gain),
            ("up", up_in, up_weight),
            ("down", down_in, down_weight),
            ("scale", scale_in, scale1),
            ("down_gain", down_gain_in, down_gain),
            ("ds", ds_in, ds_weight),
            ("head", head_in_t, head_weight),
        )
    ):
        loads[name] = pltpu.make_async_copy(source, target, local.at[k])
        loads[name].start()

    count = [0]

    def ship(source, target, peer):
        k = count[0]
        count[0] += 1
        copy = pltpu.make_async_remote_copy(
            src_ref=source,
            dst_ref=target,
            send_sem=send.at[k],
            recv_sem=recv.at[k],
            device_id=peer,
            device_id_type=MESH,
        )
        copy.start()
        return copy

    def settle(copies):
        for copy in copies:
            copy.wait()

    wide_merged[...] = jnp.zeros((CELLS, WIDE), BF16)
    wide_normed[...] = jnp.zeros((CELLS, WIDE), BF16)
    wide_branch[...] = jnp.zeros((CELLS, WIDE), BF16)
    tap_grad[...] = jnp.zeros_like(tap_grad)
    rows_ud[...] = jnp.zeros_like(rows_ud)
    padded[:, 0:8, :] = jnp.zeros((ROWS, 8, C1), F32)
    padded[:, 8 + COLS :, :] = jnp.zeros((ROWS, 8, C1), F32)
    loads["table"].wait()
    hidden_pick = one_hot(table[0:1, :], F1)
    loads["up"].wait()
    up_ordered[...] = dot_nn(up_weight[...], hidden_pick).astype(BF16)
    loads["down"].wait()
    down_ordered[...] = dot_nn(down_weight[...], hidden_pick).astype(BF16)
    unit_pick[...] = one_hot(table[1:2, 0:C2], C2)
    feature_pick[...] = one_hot(table[4:5, 0:512], 48)
    fold[...] = one_hot(table[9:10, 0:C2], 128)
    for k, row in enumerate((2, 3, 6, 7)):
        slot_pick[k] = one_hot(table[row : row + 1, 0:256], C1)
    i0 = lax.broadcasted_iota(jnp.int32, (128, 128), 0)
    i1 = lax.broadcasted_iota(jnp.int32, (128, 128), 1)
    column_pick[...] = (i1 == 4 * (i0 & 31) + (i0 >> 5)).astype(F32).astype(BF16)
    loads["taps"].wait()
    taps_ref[...] = taps[...].astype(F32)
    loads["images"].wait()
    loads["delta"].wait()
    own_pixels[...] = (own_images[...].astype(F32) + own_delta[...]).astype(BF16)
    pl.semaphore_wait(barrier, len(peers))

    sent = []
    for t in range(1, 4):
        peer = strip_peer(t)
        sent.append(ship(own_pixels.at[peer], pixels.at[strip], (dp, peer)))
    pixels[strip] = own_pixels[strip]
    for name in (
        "label", "head_gain", "stem", "stem_gain", "norm1", "scale", "down_gain", "ds", "head"
    ):
        loads[name].wait()
    settle(sent)

    perturbed = pixels[...].astype(F32).reshape(96, 128)
    perturbed = jnp.concatenate([perturbed, jnp.zeros((32, 128), F32)], axis=0).astype(BF16)
    columns = dot_nt(column_pick[...], perturbed)
    columns = jnp.concatenate([columns[32 * k : 32 * k + 32] for k in range(4)], axis=1)
    row_of = table[5:6, 0:512]
    cells = jnp.concatenate(
        [jnp.where(row_of == r, columns, 0.0) for r in range(ROWS)], axis=0
    ).astype(BF16)
    patches = dot_nt(cells, feature_pick[...]).astype(BF16)

    stem_pre = dot_nn(patches, stem_weight[...])
    stem_unit, stem_root = norm_parts(stem_pre)
    stem_out = (stem_unit * stem_gain[...]).astype(BF16).astype(F32)

    def spread_columns(values):
        padded[:, 8 : 8 + COLS, :] = values.reshape(ROWS, COLS, C1)
        for j in range(KS):
            shifted[j] = padded[:, 5 + j : 5 + j + COLS, :]

    tiles = (slice(0, 128), slice(128, C1))

    def correlate(tap_of):
        for lanes in tiles:
            totals = [None] * ROWS
            for j in range(KS):
                column = [taps_ref[tap_of(i, j) : tap_of(i, j) + 1, lanes] for i in range(KS)]
                for k in range(ROWS):
                    values = shifted[j, k, :, lanes]
                    for i in range(KS):
                        r = k - i + 3
                        if 0 <= r < ROWS:
                            term = values * column[i]
                            totals[r] = term if totals[r] is None else totals[r] + term
            for r in range(ROWS):
                mixed_ref[r, :, lanes] = totals[r]
        return mixed_ref[...].reshape(CELLS, C1)

    spread_columns(stem_out)
    mixed = correlate(lambda i, j: KS * i + j)

    mixed_unit, mixed_root = norm_parts(mixed)
    normed = (mixed_unit * norm1_gain[...]).astype(BF16)
    wide_normed[:, 0:C1] = normed
    upper = dot_nn(normed, up_ordered[...])
    half = 0.5 + 0.5 * lax.erf(upper * (0.5**0.5))
    hidden = (upper * half).astype(BF16)
    gelu_slope = half + upper * jnp.exp(-0.5 * upper * upper) * ((2.0 * np.pi) ** -0.5)
    branch = dot_nt(hidden, down_ordered[...])
    section = (stem_out + scale1[...] * branch).astype(BF16).astype(F32)

    section_unit, section_root = norm_parts(section)
    wide_merged[:, 0:C1] = (section_unit * down_gain[...]).astype(BF16)
    p0 = lax.broadcasted_iota(jnp.int32, (16, CELLS), 0)
    p1 = lax.broadcasted_iota(jnp.int32, (16, CELLS), 1)
    place_pick = (p0 == 2 * ((p1 >> 5) & 1) + (p1 & 1)).astype(F32).astype(BF16)
    merged_sum = dot_nn(place_pick, wide_merged[...])
    sums_high = merged_sum.astype(BF16).astype(F32)
    rest = merged_sum - sums_high
    sums_mid = rest.astype(BF16).astype(F32)
    sums_low = rest - sums_mid
    row16 = lax.broadcasted_iota(jnp.int32, (16, WIDE), 0)

    def place_rows(place):
        high = sums_high[place : place + 1]
        mid = sums_mid[place : place + 1]
        lowest = sums_low[place : place + 1]
        return jnp.where(
            row16 == 0, high, jnp.where(row16 == 1, mid, jnp.where(row16 == 2, lowest, 0.0))
        ).astype(BF16)

    split_sums = [place_rows(place) for place in range(4)]
    pooled = None
    for place in range(4):
        term = dot_nn(split_sums[place][:, 0:C1], ds_weight[place * C1 : (place + 1) * C1, :])
        pooled = term if pooled is None else pooled + term
    cells_two = CELLS // 4
    pooled = jnp.sum(pooled, axis=0, keepdims=True) * (1.0 / cells_two)
    pooled = jnp.broadcast_to(pooled, (16, C2))
    head_unit, head_root = norm_parts(pooled)
    gain = head_gain[...].reshape(1, C2)
    head_in = (head_unit * gain).astype(BF16)
    logits = dot_nt(head_in, head_weight[...])
    onehot = (lax.broadcasted_iota(jnp.int32, logits.shape, 1) == label[0]).astype(F32)
    top = jnp.max(logits, axis=-1, keepdims=True)
    raised = jnp.exp(logits - top)
    mass = jnp.sum(raised, axis=-1, keepdims=True)
    losses = jnp.log(mass) + top - jnp.sum(onehot * logits, axis=-1, keepdims=True)
    misc[3] = jnp.broadcast_to(losses[0:8], (8, 128))
    grad_logits = (raised / mass - onehot).astype(BF16)
    grad_head_in = dot_nn(grad_logits, head_weight[...])
    grad_pooled = norm_back(head_unit, head_root, grad_head_in * gain)
    grad_start = (grad_pooled * (1.0 / cells_two)).astype(BF16)

    block_of = lax.broadcasted_iota(jnp.int32, (16, C2), 0) == table[8:9, 0:C2]
    start_rows = jnp.where(block_of, dot_nn(grad_start, unit_pick[...]), 0.0).astype(BF16)
    start_blocks = dot_nt(start_rows, fold[...])
    head_rows = jnp.where(block_of, dot_nn(head_in, unit_pick[...]), 0.0).astype(BF16)
    head_blocks = dot_nt(head_rows, fold[...])
    e0 = lax.broadcasted_iota(jnp.int32, (CLASSES, 128), 0)
    e1 = lax.broadcasted_iota(jnp.int32, (CLASSES, 128), 1)
    logit_row = dot_nn(grad_logits, (e0 == e1).astype(F32).astype(BF16))[0:1]
    row8 = lax.broadcasted_iota(jnp.int32, (8, 128), 0)
    for hi in range(NXH):
        for k in range(NY):
            at = hi * NY + k
            third = jnp.where(row8 == 2, logit_row + head_blocks[at : at + 1], 0.0)
            for place in range(4):
                second = merged_sum[place : place + 1, 128:256] + start_blocks[at : at + 1]
                first = merged_sum[place : place + 1, 0:128]
                factors[place, hi, k] = jnp.where(row8 == 0, first, jnp.where(row8 == 1, second, third))
    mine = (x * NY + y) * NC + core
    factor_copies = []
    for step in plane_steps:
        other_lo, other_hi, other_y, same, crossed = plane_peer(step)
        for other_core, peer in ((core, same), (1 - core, crossed)):
            source = factors.at[other_lo * NC + other_core, other_hi, other_y]
            factor_copies.append(ship(source, got_factors.at[mine], peer))
    partner = (dp, x_lo * NC + (1 - core))
    source = factors.at[x_lo * NC + (1 - core), x_hi, y]
    factor_copies.append(ship(source, got_factors.at[mine], partner))
    got_factors[mine] = factors[strip, x_hi, y]

    def store_rows(blocks, at_strip, grads):
        for hi in range(NXH):
            for k in range(NY):
                at = (hi * NY + k) * PIECE
                block = grads[at : at + PIECE]
                folded = jnp.concatenate([block[0:24, 128:C1], block[24:48, 128:C1]], axis=1)
                blocks[at_strip, hi, k] = jnp.concatenate([block[:, 0:128], folded], axis=0).astype(BF16)

    def core_start(*pairs):
        copies = []
        for lo in range(NXL):
            for source, target in pairs:
                copies.append(ship(source.at[lo * NC + (1 - core)], target.at[lo], partner))
        return copies

    def core_sum(own, got, held):
        for lo in range(NXL):
            block = own[lo * NC + core].astype(F32) + got[lo].astype(F32)
            held[lo] = block.astype(BF16)

    def plane_start(held, got):
        copies = []
        for k, step in enumerate(plane_steps):
            other_lo, other_hi, other_y, peer, _ = plane_peer(step)
            copies.append(ship(held.at[other_lo, other_hi, other_y], got.at[k], peer))
        return copies

    def plane_sum(held, got, rows):
        total = held[x_lo, x_hi, y].astype(F32)
        for k in range(len(plane_steps)):
            total = total + got[k].astype(F32)
        rows[:, 0:128] = total[0:48]
        rows[0:24, 128:C1] = total[48:72, 0:64]
        rows[24:48, 128:C1] = total[48:72, 64:128]

    place_grads = [
        dot_nt(grad_start, ds_weight[place * C1 : (place + 1) * C1, :])[0:1] * down_gain[...]
        for place in range(4)
    ]
    even = (lax.broadcasted_iota(jnp.int32, (COLS, C1), 0) & 1) == 0
    by_row = [
        jnp.where(even, place_grads[2 * k], place_grads[2 * k + 1]) for k in range(2)
    ]
    grad_unit = jnp.concatenate([by_row[r % 2] for r in range(ROWS)], axis=0)
    grad_block = norm_back(section_unit, section_root, grad_unit).astype(BF16).astype(F32)

    grad_branch = (grad_block * scale1[...]).astype(BF16)
    wide_branch[:, 0:C1] = grad_branch
    grad_down = dot_tn(hidden, wide_branch[...])
    store_rows(ud, 2, grad_down[0:384])
    store_rows(ud, 3, grad_down[384:768])
    grad_hidden = dot_nn(grad_branch, down_ordered[...])
    grad_upper = (grad_hidden * gelu_slope).astype(BF16)
    grad_up = dot_tn(grad_upper, wide_normed[...])
    store_rows(ud, 0, grad_up[0:384])
    store_rows(ud, 1, grad_up[384:768])
    core_ud = core_start((ud, c_ud))

    grad_normed = dot_nt(grad_upper, up_ordered[...])
    grad_mixed = norm_back(mixed_unit, mixed_root, grad_normed * norm1_gain[...])

    mixed_ref[...] = grad_mixed.reshape(ROWS, COLS, C1)
    for lanes in tiles:
        grads = [mixed_ref[r, :, lanes] for r in range(ROWS)]
        for j in range(KS):
            totals = [None] * KS
            for k in range(ROWS):
                values = shifted[j, k, :, lanes]
                for i in range(KS):
                    r = k - i + 3
                    if 0 <= r < ROWS:
                        term = values * grads[r]
                        term = (term[0:8] + term[8:16]) + (term[16:24] + term[24:32])
                        totals[i] = term if totals[i] is None else totals[i] + term
            for i in range(KS):
                tap = KS * i + j
                tap_grad[tap : tap + 1, lanes] = jnp.sum(totals[i], axis=0, keepdims=True)

    settle(core_ud)
    core_sum(ud, c_ud, h_ud)
    plane_ud = plane_start(h_ud, x_ud)

    spread_columns(grad_mixed)
    grad_stem = grad_block + correlate(lambda i, j: KS * (KS - 1 - i) + (KS - 1 - j))
    grad_pre = norm_back(stem_unit, stem_root, grad_stem * stem_gain[...]).astype(BF16)

    grad_patches = dot_nt(grad_pre, stem_weight[...]).astype(BF16)
    grad_cells = dot_nn(grad_patches, feature_pick[...])
    grad_columns = None
    for r in range(ROWS):
        term = jnp.where(row_of == r, grad_cells[r * COLS : (r + 1) * COLS], 0.0)
        grad_columns = term if grad_columns is None else grad_columns + term
    grad_columns = grad_columns.astype(BF16)
    grad_pixels = None
    for k in range(4):
        term = dot_tn(
            grad_columns[:, 128 * k : 128 * k + 128], column_pick[32 * k : 32 * k + 32, :]
        )
        grad_pixels = term if grad_pixels is None else grad_pixels + term
    delta_grad[...] = grad_pixels[0:96].reshape(4, 24, 128).astype(BF16)

    stem_low = dot_tn(patches, grad_pre)
    stem_low = jnp.concatenate([stem_low, jnp.zeros((16, C1), F32)], axis=0).astype(BF16)
    tap_low = tap_grad[...].astype(BF16)
    slots = []
    for k in range(2):
        slots.append(dot_nn(stem_low, slot_pick[2 * k]) + dot_nn(tap_low, slot_pick[2 * k + 1]))
    paired = jnp.concatenate(slots, axis=0).T
    small[...] = paired.reshape(4, NXH, NY, NZ, 128)
    core_small = core_start((small, c_small), (delta_grad, c_delta))

    settle(core_small)
    for lo in range(NXL):
        mine = lo * NC + core
        block = delta_grad[mine].astype(F32) + c_delta[lo].astype(F32)
        late = small[mine] + c_small[lo]
        for hi in range(NXH):
            for k in range(NY):
                h_late[lo, hi, k] = jnp.concatenate([block, late[hi, k]], axis=0).astype(BF16)
    plane_late = []
    mine = x * NY + y
    for step in plane_steps:
        other_lo, other_hi, other_y, peer, _ = plane_peer(step)
        plane_late.append(ship(h_late.at[other_lo, other_hi, other_y], x_late.at[mine], peer))
    x_late[mine] = h_late[x_lo, x_hi, y]

    settle(factor_copies)
    low_half, high_half = got_factors[:, 0, :], got_factors[:, 1, :]
    third = got_factors[:, 2, :]
    first_lanes = lax.broadcasted_iota(jnp.int32, high_half.shape, 1) < 64
    sums = jnp.concatenate([low_half, jnp.where(first_lanes, high_half, 0.0)], axis=1)
    sums_high = sums.astype(BF16)
    sums_low = (sums - sums_high.astype(F32)).astype(BF16)
    starts = high_half.astype(BF16)
    o0 = lax.broadcasted_iota(jnp.int32, (128, WIDE), 0)
    o1 = lax.broadcasted_iota(jnp.int32, (128, WIDE), 1)
    head_offset = ((o1 == o0 + C1) & (o0 < 64)).astype(F32).astype(BF16)
    third = third.astype(BF16)
    placed_logits = dot_nn(third, head_offset).astype(BF16)
    products = dot_tn(starts, sums_high) + dot_tn(starts, sums_low) + dot_tn(third, placed_logits)
    rows_ds[...] = products[64 : 64 + PIECE]
    stage[:, 12:16] = jnp.zeros((NZ, 4, WIDE), F32)
    for k in range(NZ):
        stage[k, 0:6] = rows_ds[6 * k : 6 * k + 6]
    settle(plane_ud)
    plane_sum(h_ud, x_ud, rows_ud)
    for k in range(NZ):
        stage[k, 6:12] = rows_ud[6 * k : 6 * k + 6]
    settle(plane_late)
    total = x_late[0].astype(F32)
    for k in range(1, NX * NY):
        total = total + x_late[k].astype(F32)
    rows_late[...] = total[24:32]
    low_delta[z] = total[0:24].astype(BF16)
    for k in range(NZ):
        stage[k, 12:13, 0:128] = rows_late[k : k + 1]
    low[...] = stage[...].astype(BF16)

    sent = []
    for t in (4, 3, 5, 2, 6, 1, 7):
        other, peer = z_peer(t)
        sent.append(ship(low_delta.at[z], low_delta.at[z], peer))
        sent.append(ship(low.at[other], got_z.at[t - 1], peer))
    settle(sent)
    total = stage[z]
    for t in range(NZ - 1):
        total = total + got_z[t].astype(F32)
    shares[strip] = total.astype(BF16)
    total = low_delta[0].astype(F32)
    for k in range(1, NZ):
        total = total + low_delta[k].astype(F32)
    square = total * total
    for channel in range(3):
        misc[channel] = total[8 * channel : 8 * channel + 8]
    misc[4 + strip] = square[0:8] + square[8:16] + square[16:24]

    sent = []
    for t in range(1, 4):
        peer = (dp, strip_peer(t))
        sent.append(ship(shares.at[strip], shares.at[strip], peer))
        sent.append(ship(misc.at[4 + strip], misc.at[4 + strip], peer))
    settle(sent)


N_COPIES = 3 + 31 + 2 + 4 + 2 * 15 + 14 + 6
N_LOADS = 15


def finish_kernel(
    levels,
    shares,
    misc,
    perturbation,
    loss_out,
    new_out,
    stem_out,
    dw_out,
    up_out,
    down_out,
    ds_out,
    head_out,
):
    loss_out[0] = misc[3][0, 0]
    share = [shares[place].astype(F32) for place in range(4)]
    total = jnp.sum((misc[4] + misc[5]) + (misc[6] + misc[7]))
    spread = jnp.sqrt(jnp.full((8, 128), total, F32) * (1.0 / 12288) + EPS_ROOT)
    for channel in range(3):
        level = STEP_UNIT * levels[channel].astype(F32)
        step = level * misc[channel] / spread
        new_out[channel] = jnp.clip(perturbation[channel] + step, -BOUND, BOUND)
    up_out[0:6] = share[0][6:12, 0:C1]
    up_out[6:12] = share[1][6:12, 0:C1]
    down_out[0:6] = share[2][6:12, 0:C1]
    down_out[6:12] = share[3][6:12, 0:C1]
    for place in range(4):
        ds_out[:, place * C1 : (place + 1) * C1] = share[place][0:6, 0:C1]
    head_out[...] = share[0][0:6, C1 : C1 + CLASSES]
    stem_out[0:1] = share[0][12:13, 0:48]
    stem_out[1:2] = share[0][12:13, 64 : 64 + 48]
    stem_out[2:3] = share[1][12:13, 0:48]
    dw_out[0:1] = share[1][12:13, 64 : 64 + 49]
    dw_out[1:2] = share[2][12:13, 0:49]
    dw_out[2:3] = share[2][12:13, 64 : 64 + 49]


VMEM = pl.BlockSpec(memory_space=pltpu.VMEM)
SMEM = pl.BlockSpec(memory_space=pltpu.SMEM)
ANY = pl.BlockSpec(memory_space=pl.ANY)


def shaped(shape, dtype):
    return jax.ShapeDtypeStruct(shape, dtype)


def run_step(*operands):
    strips = NXL * NC
    f32 = lambda *shape: pltpu.VMEM(shape, F32)
    bf16 = lambda *shape: pltpu.VMEM(shape, BF16)
    scratch = [
        pltpu.SMEM((1,), jnp.int32),
        f32(C2),
        bf16(4, 3, 8, 128),
        f32(3, 8, 128),
        bf16(4, 3, 8, 128),
        bf16(4, 3, 8, 128),
        pltpu.VMEM((16, F1), jnp.int32),
        bf16(48, C1),
        f32(1, C1),
        bf16(KS * KS, C1),
        f32(1, C1),
        bf16(C1, F1),
        bf16(C1, F1),
        f32(1, C1),
        f32(1, C1),
        bf16(4 * C1, C2),
        bf16(CLASSES, C2),
        f32(ROWS, COLS + 16, C1),
        f32(KS, ROWS, COLS, C1),
        f32(ROWS, COLS, C1),
        bf16(CELLS, WIDE),
        bf16(CELLS, WIDE),
        bf16(CELLS, WIDE),
        f32(64, C1),
        f32(KS * KS, C1),
        bf16(C1, F1),
        bf16(C1, F1),
        bf16(C2, C2),
        bf16(128, 128),
        bf16(48, 512),
        bf16(128, C2),
        bf16(4, C1, 256),
    ]
    plane = NX * NY
    scratch += [f32(strips, NXH, NY, 8, 128)]
    for count in (strips, NXL):
        scratch += [bf16(count, NXH, NY, FOLDED, 128)]
        scratch += [f32(count, NXH, NY, NZ, 128), bf16(count, 24, 128)]
    scratch += [bf16(NXL, NXH, NY, FOLDED, 128), bf16(NXL, NXH, NY, 32, 128)]
    scratch += [f32(plane * NC, 8, 128), bf16(plane - 1, FOLDED, 128), bf16(plane, 32, 128)]
    scratch += [f32(PIECE, WIDE)] * 2 + [f32(NZ, 128)]
    scratch += [f32(NZ, 16, WIDE), bf16(NZ, 16, WIDE), bf16(NZ - 1, 16, WIDE), bf16(NZ, 24, 128)]
    scratch += [
        pltpu.SemaphoreType.DMA((N_LOADS,)),
        pltpu.SemaphoreType.DMA((N_COPIES,)),
        pltpu.SemaphoreType.DMA((N_COPIES,)),
    ]
    return pl.pallas_call(
        step_kernel,
        name="image_step_and_reduce",
        out_shape=(shaped((4, 16, WIDE), BF16), shaped((8, 8, 128), F32)),
        in_specs=[ANY] * len(operands),
        out_specs=(VMEM, VMEM),
        scratch_shapes=scratch,
        compiler_params=pltpu.CompilerParams(
            collective_id=0, has_side_effects=True, vmem_limit_bytes=60 * 1024 * 1024
        ),
    )(*operands)


def run_finish(levels, shares, misc, perturbation):
    return pl.pallas_call(
        finish_kernel,
        name="finish",
        out_shape=(
            shaped((1,), F32),
            shaped((3, 8, 128), F32),
            shaped((3, 48), F32),
            shaped((3, KS * KS), F32),
            shaped((12, C1), F32),
            shaped((12, C1), F32),
            shaped((6, 4 * C1), F32),
            shaped((6, CLASSES), F32),
        ),
        in_specs=[SMEM] + [VMEM] * 3,
        out_specs=(SMEM,) + (VMEM,) * 7,
    )(levels, shares, misc, perturbation)


def on_device(
    images,
    perturbation,
    labels,
    step_levels,
    stem_weight,
    stem_gain,
    dw1_kernel,
    norm1_gain,
    up1_weight,
    down1_weight,
    scale1,
    down_gain,
    ds_weight,
    head_gain,
    head_weight,
):
    shares, misc = run_step(
        labels,
        head_gain,
        images,
        perturbation,
        jnp.asarray(index_table()),
        stem_weight,
        stem_gain.reshape(1, C1),
        dw1_kernel,
        norm1_gain.reshape(1, C1),
        up1_weight,
        down1_weight.T,
        scale1.reshape(1, C1),
        down_gain.reshape(1, C1),
        ds_weight,
        head_weight.T,
    )
    loss, new_delta, stem, dw, up, down, ds, head = run_finish(
        step_levels, shares, misc, perturbation
    )
    return (new_delta, loss, stem.T, dw.T, up.T, down, ds.T, head)


def solution(mesh):
    return jax.shard_map(
        on_device,
        mesh=mesh,
        in_specs=(
            P("dp", None, "strip", None),
            P(None, "strip", None),
            P(("dp", "strip")),
        )
        + (P(),) * 12,
        out_specs=(
            P(None, "strip", None),
            P(("dp", "strip")),
            P(None, "dp"),
            P(None, "dp"),
            P(None, "dp"),
            P("dp", None),
            P(None, "dp"),
            P("dp", None),
        ),
        check_vma=False,
    )
```
